256 devices in a mesh: dp: 32 (over x, z), rows: 8 (over y, core).
Axes of the slice: x: 4, y: 4, z: 8, core: 2. Of those that a mesh axis runs over, the one named last changes fastest.
Arguments:
- activations: bfloat16 [65536, 8192], P('dp', 'rows'), may hold values from -6 to 6
- key_grads: bfloat16 [65536, 1024], P('dp'), may hold values from -0.125 to 0.125
- momentum: float32 [32, 8192, 1024], P('dp', 'rows'), may hold values from -6 to 6
- basis: float32 [1024, 128], replicated, may hold values from -0.1875 to 0.1875
Outputs:
- new_momentum: float32 [32, 8192, 1024], P('dp', 'rows')
- new_basis: float32 [1024, 128], P('rows')
- update: bfloat16 [8192, 1024], P(('rows', 'dp'))
The draws below stay inside these ranges and needn't reach their ends.
All inputs are finite; a program needn't handle non-finite values.
Results may differ from the reference program's by a relative error of at most 0.0015.
Values sent between devices are 32-bit elements; how exact they have to be, the bound alone decides.
A program may use at most 64 MiB of HBM per device.

```python
import math
import jax
import jax.numpy as jnp
from jax import lax

D = 8192
KV = 1024
RANK = 128
TOK_DEV = 2048
TOKENS = 65536
REPLICAS = 32
N_DP = 32


def levels(rng, extent, split, low, high):
    gain = 1.0
    for position, parts in split:
        heights = jax.random.uniform(jax.random.fold_in(jax.random.fold_in(rng, 6), position), (parts,), jnp.float32, low / len(split), high / len(split))
        gain = gain * jnp.repeat(jnp.exp(heights), extent[position] // parts).reshape((-1,) + (1,) * (len(extent) - 1 - position))
    return gain


def bell_draw(own_key, shape, deviation, most, shards=(), kind=jnp.bfloat16):
    result = jax.random.normal(own_key, shape, jnp.float32) * deviation
    if len(shards) > 0:
        result = levels(own_key, shape, shards, -0.22, 0.18) * result
    return jnp.clip(result, min=-most, max=most).astype(kind)


def setup_inputs(seed: int = 0) -> dict:
    streams_of = jax.random.split(jax.random.key(seed), 5)
    activations = bell_draw(streams_of[0], (TOKENS, D), 1.0, 6.0, ((0, 32), (1, 8)))
    key_grads = bell_draw(streams_of[1], (TOKENS, KV), TOK_DEV ** -0.5, 0.125, ((0, 32),))
    momentum = bell_draw(streams_of[2], (REPLICAS, D, KV), 1.0, 6.0, ((0, 32), (1, 8)), jnp.float32)
    basis = bell_draw(streams_of[3], (KV, RANK), KV ** -0.5, 0.1875, (), jnp.float32)
    return dict(activations=activations, key_grads=key_grads, momentum=momentum, basis=basis)


def reference(activations, key_grads, momentum, basis):
    high = lax.Precision.HIGHEST
    acts = activations.reshape(N_DP, TOK_DEV, D)
    grads = key_grads.reshape(N_DP, TOK_DEV, KV)

    def one_grad(pair):
        return lax.dot_general(pair[0].astype(jnp.float32), pair[1].astype(jnp.float32), (((0,), (0,)), ((), ())), preferred_element_type=jnp.float32)
    blended = momentum + lax.map(one_grad, (acts, grads))
    sketch = jnp.einsum('ide,er->dr', blended, basis, precision=high) / N_DP
    gram = jnp.dot(sketch.T, sketch, precision=high)
    lower = jnp.linalg.cholesky(gram)
    ortho = lax.linalg.triangular_solve(lower, sketch, left_side=False, lower=True, transpose_a=True)
    coeff = jnp.einsum('ide,dr->er', blended, ortho, precision=high) / N_DP
    feedback = jnp.dot(ortho, coeff.T, precision=high)
    new_momentum = blended - 0.2 * feedback[None]
    col_norm = jnp.sqrt(lax.optimization_barrier(jnp.sum(coeff * coeff, axis=0)) + 1e-06)
    new_basis = coeff / col_norm
    update = math.sqrt(D * KV / RANK) * jnp.dot(ortho, new_basis.T, precision=high)
    return (new_momentum, new_basis, update.astype(jnp.bfloat16))
```

```python
import functools
import math

import jax
import jax.numpy as jnp
from jax import lax
from jax.experimental import pallas as pl
from jax.experimental.pallas import tpu as pltpu
from jax.sharding import PartitionSpec as P

D = 8192
KV = 1024
RANK = 128
REPLICAS = 32
NX, NY, NZ = 4, 4, 8
TOK = 2048
ROWS = 1024
BLOCK = ROWS // NX
PIECE = BLOCK // NZ
X_ORDER = (2, 1, 3, 0)
Z_FAR = (4, 3, 5, 2, 6, 1, 7)
Z_NEAR = (1, 7, 2, 6, 3, 5, 4)
f32, bf16 = jnp.float32, jnp.bfloat16
HIGH = lax.Precision.HIGHEST
MESH = pl.DeviceIdType.MESH
TN = (((0,), (0,)), ((), ()))
NT = (((1,), (1,)), ((), ()))


def split(v):
    hi = v.astype(bf16)
    return hi, (v - hi.astype(f32)).astype(bf16)


def dot(a, b, dims=(((1,), (0,)), ((), ()))):
    return lax.dot_general(a, b, dims, preferred_element_type=f32)


def eliminate(a_ref, e_ref, first, last):
    tiles = RANK // 8
    a = {i: a_ref[8 * i : 8 * i + 8] for i in range(first // 8, tiles)}
    e = {i: e_ref[8 * i : 8 * i + 8] for i in range(first // 8, tiles)}
    below = lax.broadcasted_iota(jnp.int32, (8, 1), 0)
    for k in range(first, last):
        t, s = divmod(k, 8)
        scale = 1.0 / a[t][s : s + 1, k : k + 1]
        row_a = a[t][s : s + 1] * scale
        row_e = e[t][s : s + 1] * scale
        for i in range(t, tiles):
            m = a[i][:, k : k + 1]
            if i == t:
                if s == 7:
                    continue
                m = jnp.where(below > s, m, 0.0)
            a[i] = a[i] - m * row_a
            e[i] = e[i] - m * row_e
    for i in a:
        a_ref[8 * i : 8 * i + 8] = a[i]
        e_ref[8 * i : 8 * i + 8] = e[i]


def main_kernel(
    acts, kgrads, mom, basis,
    b_out, o_out, own_out, c_out,
    a_v, k_v, b_v, bh_v, bl_v, q_v, p_v, x_in, z_src, z_in, s_v, g_blk, g_mine, g_part, g_y,
    u_v, c_in, half, xy_in, v_in, u_all, o_v, own_v, c_v, ga, ge,
    load_sem, store_sem, send_sem, x_sem, z_sem, zag_sem, xag_sem, g_sem, gy_sem, c_sem, xy_sem, v_sem, xyag_sem, cag_sem,
):
    dp = lax.axis_index("dp")
    rows = lax.axis_index("rows")
    x, z = dp // NZ, dp % NZ
    y, core = rows // 2, rows % 2
    sends = []

    def device(xo=0, yo=0, zo=0, flip=False):
        c = 1 - core if flip else core
        return (((x + xo) % NX) * NZ + (z + zo) % NZ, ((y + yo) % NY) * 2 + c)

    def send(src, dst, sem, to):
        copy = pltpu.make_async_remote_copy(
            src_ref=src, dst_ref=dst, send_sem=send_sem.at[len(sends)], recv_sem=sem, device_id=to, device_id_type=MESH
        )
        copy.start()
        sends.append(copy)

    def arrive(dst, sem):
        pltpu.make_async_copy(dst, dst, sem).wait()

    load_a = [
        pltpu.make_async_copy(acts.at[:, pl.ds(pl.multiple_of(((x + o) % NX) * BLOCK, BLOCK), BLOCK)], a_v.at[c], load_sem.at[c])
        for c, o in enumerate(X_ORDER)
    ]
    load_m = [
        pltpu.make_async_copy(mom.at[0, pl.ds(pl.multiple_of(((x + o) % NX) * BLOCK, BLOCK), BLOCK)], b_v.at[c], load_sem.at[4 + c])
        for c, o in enumerate(X_ORDER)
    ]
    load_k = pltpu.make_async_copy(kgrads, k_v, load_sem.at[8])
    load_q = pltpu.make_async_copy(basis, q_v, load_sem.at[9])
    load_k.start()
    load_a[0].start()
    load_m[0].start()
    load_q.start()
    for c in range(1, NX):
        load_a[c].start()
        load_m[c].start()

    barrier = pltpu.get_barrier_semaphore()
    peers = [(xo, yo, 0, False) for xo in range(NX) for yo in range(NY) if (xo, yo) != (0, 0)]
    peers += [(0, 0, zo, False) for zo in range(1, NZ)] + [(0, 0, 0, True)]
    for peer in peers:
        pl.semaphore_signal(barrier, inc=1, device_id=device(*peer), device_id_type=MESH)

    stores = []
    load_q.wait()
    load_k.wait()
    qh, ql = split(q_v[...])
    q2 = jnp.concatenate([qh, ql], axis=1)
    for c, o in enumerate(X_ORDER):
        load_a[c].wait()
        load_m[c].wait()
        b = b_v[c] + dot(a_v[c], k_v[...], TN)
        b_v[c] = b
        bh, bl = split(b)
        bh_v[c] = bh
        bl_v[c] = bl
        two = dot(bh, q2)
        p_v[c] = two[:, :RANK] + (two[:, RANK:] + dot(bl, qh))
        if c == 0:
            pl.semaphore_wait(barrier, len(peers))
        if o:
            send(p_v.at[c], x_in.at[o - 1], x_sem, device(xo=o))
        at = pl.ds(pl.multiple_of(((x + o) % NX) * BLOCK, BLOCK), BLOCK)
        stores.append(pltpu.make_async_copy(b_v.at[c], b_out.at[at], store_sem.at[c]))
        stores[-1].start()

    arrive(x_in, x_sem)
    z_src[...] = (p_v[3] + x_in[0]) + (x_in[1] + x_in[2])
    for o in Z_FAR:
        at = pl.ds(pl.multiple_of(((z + o) % NZ) * PIECE, PIECE), PIECE)
        send(z_src.at[at], z_in.at[o - 1], z_sem, device(zo=o))
    mine = z_src[pl.ds(pl.multiple_of(z * PIECE, PIECE), PIECE)]
    arrive(z_in, z_sem)
    for o in range(NZ - 1):
        mine = mine + z_in[o]
    own_v[...] = mine * (1.0 / REPLICAS)
    s_v[0, z] = own_v[...]

    for o in Z_FAR:
        send(own_v, s_v.at[0, z], zag_sem.at[o - 1], device(zo=o))
    for xo in (2, 1, 3):
        send(own_v, s_v.at[NX - xo, z], xag_sem.at[NX - xo - 1], device(xo=xo))
    for o in Z_NEAR:
        at = (z + NZ - o) % NZ
        arrive(s_v.at[0, at], zag_sem.at[o - 1])
        for xo in (2, 1, 3):
            send(s_v.at[0, at], s_v.at[NX - xo, at], xag_sem.at[NX - xo - 1], device(xo=xo))

    for n, o in enumerate((0, 1, 3, 2)):
        if o:
            arrive(s_v.at[o], xag_sem.at[o - 1])
        c = X_ORDER.index(o)
        s = s_v[o].reshape(BLOCK, RANK)
        g_blk[(x + o) % NX] = lax.dot_general(s, s, TN, precision=HIGH, preferred_element_type=f32)
        if n == NX - 1:
            g_mine[...] = (g_blk[0] + g_blk[1]) + (g_blk[2] + g_blk[3])
            send(g_mine, g_part, g_sem, device(flip=True))
        sh, sl = split(s)
        two = dot(jnp.concatenate([sh, sl], axis=1), bh_v[c], TN)
        u = two[:RANK] + (two[RANK:] + dot(sh, bl_v[c], TN))
        for b in range(8):
            blk = u[:, 128 * b : 128 * b + 128]
            u_v[b] = blk if n == 0 else u_v[b] + blk

    send(u_v.at[pl.ds(4 * (1 - core), 4)], c_in, c_sem, device(flip=True))
    arrive(g_part, g_sem)
    g_y[y] = g_mine[...] + g_part[...]
    for yo in (2, 1, 3):
        send(g_y.at[y], g_y.at[y], gy_sem.at[yo - 1], device(yo=yo))
    arrive(c_in, c_sem)
    for b in range(4):
        tot = u_v[4 * core + b] + c_in[b]
        for r in range(4):
            half[4 * b + r] = tot[32 * r : 32 * r + 32]
    order = sorted(((xo, yo) for xo in range(NX) for yo in range(NY) if (xo, yo) != (0, 0)), key=lambda o: -min(o[0], NX - o[0]) - min(o[1], NY - o[1]))
    for xo, yo in order:
        p = ((x + xo) % NX) * NY + (y + yo) % NY
        send(half.at[p], xy_in.at[xo * NY + yo - 1], xy_sem, device(xo=xo, yo=yo))
    me = x * NY + y
    tot = half[me]
    arrive(xy_in, xy_sem)
    for o in range(NX * NY - 1):
        tot = tot + xy_in[o]
    v_in[z] = tot
    for o in Z_FAR:
        send(v_in.at[z], v_in.at[z], v_sem.at[o - 1], device(zo=o))
    for yo in range(1, NY):
        arrive(g_y.at[(y + NY - yo) % NY], gy_sem.at[yo - 1])
    ga[...] = (g_y[0] + g_y[1]) + (g_y[2] + g_y[3])
    ge[...] = (lax.broadcasted_iota(jnp.int32, (RANK, RANK), 0) == lax.broadcasted_iota(jnp.int32, (RANK, RANK), 1)).astype(f32)
    eliminate(ga, ge, 0, 64)
    for o in range(1, NZ):
        arrive(v_in.at[(z + NZ - o) % NZ], v_sem.at[o - 1])
    tot = v_in[0]
    for o in range(1, NZ):
        tot = tot + v_in[o]
    u_all[16 * core + me] = tot
    for xo, yo in order:
        at = 16 * core + me
        send(u_all.at[at], u_all.at[at], xyag_sem.at[xo * NY + yo - 1], device(xo=xo, yo=yo))
    send(u_all.at[16 * core + me], u_all.at[16 * core + me], cag_sem, device(flip=True))
    eliminate(ga, ge, 64, RANK)
    a = ga[...]
    eye = lax.broadcasted_iota(jnp.int32, (RANK, RANK), 0) == lax.broadcasted_iota(jnp.int32, (RANK, RANK), 1)
    pivots = jnp.sum(jnp.where(eye, a, 0.0), axis=1, keepdims=True)
    inverse = ge[...] / jnp.sqrt(pivots)
    for c, o in enumerate(X_ORDER):
        o_v[c] = lax.dot_general(s_v[o].reshape(BLOCK, RANK), inverse, NT, precision=HIGH, preferred_element_type=f32)
        at = pl.ds(pl.multiple_of(((x + o) % NX) * BLOCK, BLOCK), BLOCK)
        stores.append(pltpu.make_async_copy(o_v.at[c], o_out.at[at], store_sem.at[4 + c]))
        stores[-1].start()
    own_rows = pltpu.make_async_copy(o_v.at[3, pl.ds(pl.multiple_of(z * PIECE, PIECE), PIECE)], own_out, store_sem.at[8])
    own_rows.start()
    stores.append(own_rows)
    for xo, yo in reversed(order):
        at = 16 * core + ((x + NX - xo) % NX) * NY + (y + NY - yo) % NY
        arrive(u_all.at[at], xyag_sem.at[xo * NY + yo - 1])
        send(u_all.at[at], u_all.at[at], cag_sem, device(flip=True))
    arrive(u_all.at[pl.ds(16 * (1 - core), 16)], cag_sem)
    for b in range(8):
        ut = u_all[4 * b : 4 * b + 4].reshape(RANK, 128)
        c_v[b] = jnp.dot(inverse, ut, precision=HIGH, preferred_element_type=f32) * (1.0 / REPLICAS)
    stores.append(pltpu.make_async_copy(c_v, c_out, store_sem.at[9]))
    stores[-1].start()
    for copy in sends:
        copy.wait_send()
    for copy in stores:
        copy.wait()


def final_kernel(b_ref, o_ref, own_ref, c_ref, new_ref, basis_ref, upd_ref, ch_v, cl_v, n_v):
    @pl.when(pl.program_id(0) == 0)
    def _():
        squares = c_ref[0] * c_ref[0]
        for b in range(1, 8):
            squares = squares + c_ref[b] * c_ref[b]
        norm = jnp.sqrt(jnp.sum(squares, axis=1, keepdims=True) + 1e-06)
        own_h, own_l = split(own_ref[...])
        for b in range(8):
            cols = slice(128 * b, 128 * b + 128)
            ch, cl = split(c_ref[b])
            ch_v[:, cols] = ch
            cl_v[:, cols] = cl
            n_v[b] = c_ref[b] / norm
            nh, nl = split(n_v[b])
            upd = dot(own_h, nh) + (dot(own_h, nl) + dot(own_l, nh))
            upd_ref[:, cols] = (math.sqrt(D * KV / RANK) * upd).astype(bf16)
        basis_ref[...] = n_v[lax.axis_index("rows")].T

    oh, ol = split(o_ref[...])
    ch = ch_v[...]
    feedback = dot(oh, ch) + (dot(oh, cl_v[...]) + dot(ol, ch))
    new_ref[0] = b_ref[...] - 0.2 * feedback


def body(activations, key_grads, momentum, basis):
    hbm = pl.BlockSpec(memory_space=pl.ANY)
    sds = jax.ShapeDtypeStruct
    dma = lambda *n: pltpu.SemaphoreType.DMA(n)
    b, o, own, c = pl.pallas_call(
        main_kernel,
        out_shape=(sds((ROWS, KV), f32), sds((ROWS, RANK), f32), sds((PIECE, RANK), f32), sds((8, RANK, 128), f32)),
        in_specs=[pl.BlockSpec(memory_space=pltpu.HBM)] * 4,
        out_specs=(hbm,) * 4,
        scratch_shapes=[
            pltpu.VMEM((NX, TOK, BLOCK), bf16),
            pltpu.VMEM((TOK, KV), bf16),
            pltpu.VMEM((NX, BLOCK, KV), f32),
            pltpu.VMEM((NX, BLOCK, KV), bf16),
            pltpu.VMEM((NX, BLOCK, KV), bf16),
            pltpu.VMEM((KV, RANK), f32),
            pltpu.VMEM((NX, BLOCK, RANK), f32),
            pltpu.VMEM((NX - 1, BLOCK, RANK), f32),
            pltpu.VMEM((BLOCK, RANK), f32),
            pltpu.VMEM((NZ - 1, PIECE, RANK), f32),
            pltpu.VMEM((NX, NZ, PIECE, RANK), f32),
            pltpu.VMEM((NX, RANK, RANK), f32),
            pltpu.VMEM((RANK, RANK), f32),
            pltpu.VMEM((RANK, RANK), f32),
            pltpu.VMEM((NY, RANK, RANK), f32),
            pltpu.VMEM((8, RANK, 128), f32),
            pltpu.VMEM((4, RANK, 128), f32),
            pltpu.VMEM((16, 32, 128), f32),
            pltpu.VMEM((15, 32, 128), f32),
            pltpu.VMEM((NZ, 32, 128), f32),
            pltpu.VMEM((32, 32, 128), f32),
            pltpu.VMEM((NX, BLOCK, RANK), f32),
            pltpu.VMEM((PIECE, RANK), f32),
            pltpu.VMEM((8, RANK, 128), f32),
            pltpu.VMEM((RANK, RANK), f32),
            pltpu.VMEM((RANK, RANK), f32),
            dma(10), dma(10), dma(110), pltpu.SemaphoreType.DMA, pltpu.SemaphoreType.DMA, dma(7), dma(3),
            pltpu.SemaphoreType.DMA, dma(3), pltpu.SemaphoreType.DMA, pltpu.SemaphoreType.DMA, dma(7), dma(15), pltpu.SemaphoreType.DMA,
        ],
        compiler_params=pltpu.CompilerParams(collective_id=0, has_side_effects=True, vmem_limit_bytes=40 << 20),
        name="main",
    )(*(pltpu.with_memory_space_constraint(v, pltpu.HBM) for v in (activations, key_grads, momentum, basis)))
    whole = lambda *shape: pl.BlockSpec(shape, lambda i: (0,) * len(shape))
    return pl.pallas_call(
        final_kernel,
        grid=(4,),
        out_shape=(sds((1, ROWS, KV), f32), sds((RANK, RANK), f32), sds((PIECE, KV), bf16)),
        in_specs=[
            pl.BlockSpec((256, KV), lambda i: (i, 0)),
            pl.BlockSpec((256, RANK), lambda i: (i, 0)),
            whole(PIECE, RANK),
            whole(8, RANK, 128),
        ],
        out_specs=(pl.BlockSpec((1, 256, KV), lambda i: (0, i, 0)), whole(RANK, RANK), whole(PIECE, KV)),
        scratch_shapes=[pltpu.VMEM((RANK, KV), bf16), pltpu.VMEM((RANK, KV), bf16), pltpu.VMEM((8, RANK, 128), f32)],
        compiler_params=pltpu.CompilerParams(vmem_limit_bytes=16 << 20),
        name="final",
    )(b, o, own, c)


def solution(mesh):
    in_specs = (P("dp", "rows"), P("dp", None), P("dp", "rows", None), P())
    out_specs = (P("dp", "rows", None), P("rows", None), P(("rows", "dp"), None))
    return jax.shard_map(body, mesh=mesh, in_specs=in_specs, out_specs=out_specs, check_vma=False)
```

```python
import functools
import math

import jax
import jax.numpy as jnp
from jax import lax
from jax.experimental import pallas as pl
from jax.experimental.pallas import tpu as pltpu
from jax.sharding import PartitionSpec as P

D = 8192
KV = 1024
RANK = 128
REPLICAS = 32
NX, NY, NZ = 4, 4, 8
TOK = 2048
ROWS = 1024
BLOCK = ROWS // NX
PIECE = BLOCK // NZ
X_ORDER = (2, 1, 3, 0)
Z_FAR = (4, 3, 5, 2, 6, 1, 7)
Z_NEAR = (1, 7, 2, 6, 3, 5, 4)
BEFORE_X = (0, 1, 2)
BEFORE_Z = (3,)
CUT = 72
f32, bf16 = jnp.float32, jnp.bfloat16
HIGH = lax.Precision.HIGHEST
MESH = pl.DeviceIdType.MESH
TN = (((0,), (0,)), ((), ()))
NT = (((1,), (1,)), ((), ()))


def split(v):
    hi = v.astype(bf16)
    return hi, (v - hi.astype(f32)).astype(bf16)


def dot(a, b, dims=(((1,), (0,)), ((), ()))):
    return lax.dot_general(a, b, dims, preferred_element_type=f32)


def eliminate(a_ref, e_ref, inv_ref, first, last):
    tiles = RANK // 8
    a = {i: a_ref[8 * i : 8 * i + 8] for i in range(first // 8, tiles)}
    e = {i: e_ref[8 * i : 8 * i + 8] for i in range(first // 8, tiles)}
    upper = lax.broadcasted_iota(jnp.int32, (8, 1), 0) >= 4
    for k in range(first, last, 4):
        t, s = divmod(k, 8)
        ra = [a[t][s + j : s + j + 1] for j in range(4)]
        re = [e[t][s + j : s + j + 1] for j in range(4)]
        g = {(i, j): jnp.broadcast_to(ra[i][:, k + j : k + j + 1], (1, RANK)) for i in range(4) for j in range(i, 4)}
        wa, we, low = [None] * 4, [None] * 4, {}
        for j in range(4):
            inv = 1.0 / g[j, j]
            for i in range(j + 1, 4):
                low[i, j] = g[j, i] * inv
                for m in range(i, 4):
                    g[i, m] = g[i, m] - low[i, j] * g[j, m]
            for i in range(j + 1, 4):
                ra[i] = ra[i] - low[i, j] * ra[j]
                re[i] = re[i] - low[i, j] * re[j]
            inv_ref[k + j : k + j + 1] = re[j] / jnp.sqrt(g[j, j])
            wa[j], we[j] = ra[j] * inv, re[j] * inv
        for j in (2, 1, 0):
            for i in range(j + 1, 4):
                wa[j] = wa[j] - low[i, j] * wa[i]
                we[j] = we[j] - low[i, j] * we[i]
        for i in range(t, tiles):
            if i == t and s == 4:
                continue
            m = [a[i][:, k + j : k + j + 1] for j in range(4)]
            if i == t:
                m = [jnp.where(upper, v, 0.0) for v in m]
            a[i] = a[i] - ((m[0] * wa[0] + m[1] * wa[1]) + (m[2] * wa[2] + m[3] * wa[3]))
            e[i] = e[i] - ((m[0] * we[0] + m[1] * we[1]) + (m[2] * we[2] + m[3] * we[3]))
    for i in range(last // 8, tiles):
        a_ref[8 * i : 8 * i + 8] = a[i]
        e_ref[8 * i : 8 * i + 8] = e[i]


def main_kernel(
    acts, kgrads, mom, basis,
    b_v, o_v, c_v,
    a_v, k_v, kq_v, bh_v, bl_v, q_v, p_v, x_in, z_src, z_in, s_v, s2_v, g_blk, g_mine, g_part, g_y,
    u_out, u_own, c_in, half, xy_in, v_in, u_all, own_v, ga, ge, inv_v,
    load_sem, send_sem, x_sem, z_sem, zag_sem, xag_sem, g_sem, gy_sem, c_sem, xy_sem, v_sem, xyag_sem, cag_sem,
):
    dp = lax.axis_index("dp")
    rows = lax.axis_index("rows")
    x, z = dp // NZ, dp % NZ
    y, core = rows // 2, rows % 2
    sends = []

    def device(xo=0, yo=0, zo=0, flip=False):
        c = 1 - core if flip else core
        return (((x + xo) % NX) * NZ + (z + zo) % NZ, ((y + yo) % NY) * 2 + c)

    def send(src, dst, sem, to):
        copy = pltpu.make_async_remote_copy(
            src_ref=src, dst_ref=dst, send_sem=send_sem.at[len(sends)], recv_sem=sem, device_id=to, device_id_type=MESH
        )
        copy.start()
        sends.append(copy)

    def arrive(dst, sem):
        pltpu.make_async_copy(dst, dst, sem).wait()

    quarter = TOK // 4
    load_q = pltpu.make_async_copy(basis, q_v, load_sem.at[12])
    load_k = [
        pltpu.make_async_copy(kgrads.at[pl.ds(quarter * i, quarter)], k_v.at[pl.ds(quarter * i, quarter)], load_sem.at[8 + i])
        for i in range(4)
    ]
    load_a, load_m = {}, {}
    for o in X_ORDER:
        at = pl.ds(pl.multiple_of(((x + o) % NX) * BLOCK, BLOCK), BLOCK)
        load_a[o] = pltpu.make_async_copy(acts.at[:, at], a_v.at[o], load_sem.at[o])
        load_m[o] = pltpu.make_async_copy(mom.at[0, at], b_v.at[o], load_sem.at[4 + o])
    load_q.start()
    for copy in load_k:
        copy.start()
    for o in X_ORDER:
        load_a[o].start()
        load_m[o].start()

    barrier = pltpu.get_barrier_semaphore()
    peers = [(xo, yo, 0, False) for xo in range(NX) for yo in range(NY) if (xo, yo) != (0, 0)]
    peers += [(0, 0, zo, False) for zo in range(1, NZ)] + [(0, 0, 0, True)]
    for peer in peers:
        pl.semaphore_signal(barrier, inc=1, device_id=device(*peer), device_id_type=MESH)

    load_q.wait()
    qh, ql = split(q_v[...])
    q2 = jnp.concatenate([qh, ql], axis=1)
    for i in range(4):
        load_k[i].wait()
        at = slice(quarter * i, quarter * i + quarter)
        two = dot(k_v[at], q2)
        kq_v[at, :RANK], kq_v[at, RANK:] = split(two[:, :RANK] + two[:, RANK:])
    for o in X_ORDER:
        load_a[o].wait()
        load_m[o].wait()
        mh, ml = split(b_v[o])
        two = dot(a_v[o], kq_v[...], TN) + dot(mh, q2)
        p_v[o] = two[:, :RANK] + (two[:, RANK:] + dot(ml, qh))
        if o == X_ORDER[0]:
            pl.semaphore_wait(barrier, len(peers))
        if o:
            send(p_v.at[o], x_in.at[o - 1], x_sem, device(xo=o))

    def blend(o):
        b = b_v[o] + dot(a_v[o], k_v[...], TN)
        b_v[o] = b
        bh_v[o], bl_v[o] = split(b)

    for o in BEFORE_X:
        blend(o)

    arrive(x_in, x_sem)
    z_src[...] = (p_v[0] + x_in[0]) + (x_in[1] + x_in[2])
    for o in Z_FAR:
        at = pl.ds(pl.multiple_of(((z + o) % NZ) * PIECE, PIECE), PIECE)
        send(z_src.at[at], z_in.at[o - 1], z_sem, device(zo=o))
    for o in BEFORE_Z:
        blend(o)
    mine = z_src[pl.ds(pl.multiple_of(z * PIECE, PIECE), PIECE)]
    arrive(z_in, z_sem)
    for o in range(NZ - 1):
        mine = mine + z_in[o]
    own_v[...] = mine * (1.0 / REPLICAS)
    s_v[0, z] = own_v[...]

    for o in Z_FAR:
        send(own_v, s_v.at[0, z], zag_sem.at[o - 1], device(zo=o))
    for xo in (2, 1, 3):
        send(own_v, s_v.at[NX - xo, z], xag_sem.at[NX - xo - 1], device(xo=xo))
    for o in Z_NEAR:
        at = (z + NZ - o) % NZ
        arrive(s_v.at[0, at], zag_sem.at[o - 1])
        for xo in (2, 1, 3):
            send(s_v.at[0, at], s_v.at[NX - xo, at], xag_sem.at[NX - xo - 1], device(xo=xo))

    def gram(o):
        s = s_v[o].reshape(BLOCK, RANK)
        g_blk[(x + o) % NX] = lax.dot_general(s, s, TN, precision=HIGH, preferred_element_type=f32)

    def halves(o):
        s2_v[o, :, :RANK], s2_v[o, :, RANK:] = split(s_v[o].reshape(BLOCK, RANK))

    gram(0)
    for o in (0, 1, 3, 2):
        if o:
            arrive(s_v.at[o], xag_sem.at[o - 1])
        halves(o)

    def right(dst, which):
        cols = pl.ds(pl.multiple_of(512 * which, 512), 512)
        s2 = s2_v[...].reshape(ROWS, 2 * RANK)
        big = dot(s2, bh_v[:, :, cols].reshape(ROWS, 512), TN)
        small = dot(s2[:, :RANK], bl_v[:, :, cols].reshape(ROWS, 512), TN)
        u = big[:RANK] + (big[RANK:] + small)
        for b in range(4):
            dst[b] = u[:, 128 * b : 128 * b + 128]

    right(u_out, 1 - core)
    send(u_out, c_in, c_sem, device(flip=True))
    for o in (1, 3, 2):
        gram(o)
    g_mine[...] = (g_blk[0] + g_blk[1]) + (g_blk[2] + g_blk[3])
    send(g_mine, g_part, g_sem, device(flip=True))
    right(u_own, core)
    arrive(c_in, c_sem)
    for b in range(4):
        tot = u_own[b] + c_in[b]
        for r in range(4):
            half[4 * b + r] = tot[32 * r : 32 * r + 32]
    order = sorted(
        ((xo, yo) for xo in range(NX) for yo in range(NY) if (xo, yo) != (0, 0)),
        key=lambda o: -min(o[0], NX - o[0]) - min(o[1], NY - o[1]),
    )
    for xo, yo in order:
        p = ((x + xo) % NX) * NY + (y + yo) % NY
        send(half.at[p], xy_in.at[xo * NY + yo - 1], xy_sem, device(xo=xo, yo=yo))
    arrive(g_part, g_sem)
    g_y[y] = g_mine[...] + g_part[...]
    for yo in (2, 1, 3):
        send(g_y.at[y], g_y.at[y], gy_sem.at[yo - 1], device(yo=yo))
    me = x * NY + y
    for yo in (1, 3, 2):
        arrive(g_y.at[(y + NY - yo) % NY], gy_sem.at[yo - 1])
    ga[...] = (g_y[0] + g_y[1]) + (g_y[2] + g_y[3])
    eye = lax.broadcasted_iota(jnp.int32, (RANK, RANK), 0) == lax.broadcasted_iota(jnp.int32, (RANK, RANK), 1)
    ge[...] = eye.astype(f32)
    eliminate(ga, ge, inv_v, 0, CUT)
    tot = half[me]
    arrive(xy_in, xy_sem)
    for o in range(NX * NY - 1):
        tot = tot + xy_in[o]
    v_in[z] = tot
    for o in Z_FAR:
        send(v_in.at[z], v_in.at[z], v_sem.at[o - 1], device(zo=o))
    eliminate(ga, ge, inv_v, CUT, RANK)
    for o in Z_NEAR:
        arrive(v_in.at[(z + NZ - o) % NZ], v_sem.at[o - 1])
    tot = v_in[0]
    for o in range(1, NZ):
        tot = tot + v_in[o]
    u_all[core, me] = tot
    for xo, yo in order:
        send(u_all.at[core, me], u_all.at[core, me], xyag_sem.at[xo * NY + yo - 1], device(xo=xo, yo=yo))
    send(u_all.at[core, me], u_all.at[core, me], cag_sem, device(flip=True))
    inverse = inv_v[...]
    for o in range(NX):
        o_v[o] = lax.dot_general(s_v[o].reshape(BLOCK, RANK), inverse, NT, precision=HIGH, preferred_element_type=f32)
    for xo, yo in reversed(order):
        at = ((x + NX - xo) % NX) * NY + (y + NY - yo) % NY
        arrive(u_all.at[core, at], xyag_sem.at[xo * NY + yo - 1])
        send(u_all.at[core, at], u_all.at[core, at], cag_sem, device(flip=True))

    def finish(which):
        for b in range(4):
            ut = u_all[which, pl.ds(4 * b, 4)].reshape(RANK, 128)
            c_v[4 * which + b] = jnp.dot(inverse, ut, precision=HIGH, preferred_element_type=f32) * (1.0 / REPLICAS)

    finish(core)
    arrive(u_all.at[1 - core], cag_sem)
    finish(1 - core)
    for copy in sends:
        copy.wait_send()


def final_kernel(b_ref, o_ref, c_ref, new_ref, basis_ref, upd_ref, c2_v, cl_v, n_v, new_v, basis_v, upd_v, sem):
    x, z = lax.axis_index("dp") // NZ, lax.axis_index("dp") % NZ
    squares = 0.0
    for b in range(8):
        cols = slice(128 * b, 128 * b + 128)
        v = c_ref[b]
        ch, cl_v[:, cols] = split(v)
        c2_v[:RANK, cols] = ch
        c2_v[RANK:, cols] = ch
        squares = squares + v * v
    copies = []
    for o in range(NX):
        oh, ol = split(o_ref[o])
        feedback = dot(jnp.concatenate([oh, ol], axis=1), c2_v[...]) + dot(oh, cl_v[...])
        new_v[o] = b_ref[o] - 0.2 * feedback
        at = pl.ds(pl.multiple_of(((x + o) % NX) * BLOCK, BLOCK), BLOCK)
        copies.append(pltpu.make_async_copy(new_v.at[o], new_ref.at[0, at], sem.at[o]))
        copies[-1].start()
        if o == 0:
            norm = jnp.sqrt(jnp.sum(squares, axis=1, keepdims=True) + 1e-06)
            own_h, own_l = split(o_ref[0, pl.ds(pl.multiple_of(z * PIECE, PIECE), PIECE)])
            for b in range(8):
                n_v[b] = c_ref[b] / norm
                nh, nl = split(n_v[b])
                upd = dot(own_h, nh) + (dot(own_h, nl) + dot(own_l, nh))
                upd_v[:, 128 * b : 128 * b + 128] = (math.sqrt(D * KV / RANK) * upd).astype(bf16)
            basis_v[...] = n_v[lax.axis_index("rows")].T
            copies.append(pltpu.make_async_copy(upd_v, upd_ref, sem.at[4]))
            copies[-1].start()
            copies.append(pltpu.make_async_copy(basis_v, basis_ref, sem.at[5]))
            copies[-1].start()
    for copy in copies:
        copy.wait()


def body(activations, key_grads, momentum, basis):
    hbm = pl.BlockSpec(memory_space=pl.ANY)
    vmem = pl.BlockSpec(memory_space=pltpu.VMEM)
    sds = jax.ShapeDtypeStruct
    dma = lambda *n: pltpu.SemaphoreType.DMA(n)
    one = pltpu.SemaphoreType.DMA
    b, o, c = pl.pallas_call(
        main_kernel,
        out_shape=(sds((NX, BLOCK, KV), f32), sds((NX, BLOCK, RANK), f32), sds((8, RANK, 128), f32)),
        in_specs=[pl.BlockSpec(memory_space=pltpu.HBM)] * 4,
        out_specs=(vmem,) * 3,
        scratch_shapes=[
            pltpu.VMEM((NX, TOK, BLOCK), bf16),
            pltpu.VMEM((TOK, KV), bf16),
            pltpu.VMEM((TOK, 2 * RANK), bf16),
            pltpu.VMEM((NX, BLOCK, KV), bf16),
            pltpu.VMEM((NX, BLOCK, KV), bf16),
            pltpu.VMEM((KV, RANK), f32),
            pltpu.VMEM((NX, BLOCK, RANK), f32),
            pltpu.VMEM((NX - 1, BLOCK, RANK), f32),
            pltpu.VMEM((BLOCK, RANK), f32),
            pltpu.VMEM((NZ - 1, PIECE, RANK), f32),
            pltpu.VMEM((NX, NZ, PIECE, RANK), f32),
            pltpu.VMEM((NX, BLOCK, 2 * RANK), bf16),
            pltpu.VMEM((NX, RANK, RANK), f32),
            pltpu.VMEM((RANK, RANK), f32),
            pltpu.VMEM((RANK, RANK), f32),
            pltpu.VMEM((NY, RANK, RANK), f32),
            pltpu.VMEM((4, RANK, 128), f32),
            pltpu.VMEM((4, RANK, 128), f32),
            pltpu.VMEM((4, RANK, 128), f32),
            pltpu.VMEM((16, 32, 128), f32),
            pltpu.VMEM((15, 32, 128), f32),
            pltpu.VMEM((NZ, 32, 128), f32),
            pltpu.VMEM((2, 16, 32, 128), f32),
            pltpu.VMEM((PIECE, RANK), f32),
            pltpu.VMEM((RANK, RANK), f32),
            pltpu.VMEM((RANK, RANK), f32),
            pltpu.VMEM((RANK, RANK), f32),
            dma(13), dma(110), one, one, dma(7), dma(3), one, dma(3), one, one, dma(7), dma(15), one,
        ],
        compiler_params=pltpu.CompilerParams(collective_id=0, has_side_effects=True, vmem_limit_bytes=36 << 20),
        name="main",
    )(*(pltpu.with_memory_space_constraint(v, pltpu.HBM) for v in (activations, key_grads, momentum, basis)))
    return pl.pallas_call(
        final_kernel,
        out_shape=(sds((1, ROWS, KV), f32), sds((RANK, RANK), f32), sds((PIECE, KV), bf16)),
        in_specs=[vmem] * 3,
        out_specs=(hbm,) * 3,
        scratch_shapes=[
            pltpu.VMEM((2 * RANK, KV), bf16),
            pltpu.VMEM((RANK, KV), bf16),
            pltpu.VMEM((8, RANK, 128), f32),
            pltpu.VMEM((NX, BLOCK, KV), f32),
            pltpu.VMEM((RANK, RANK), f32),
            pltpu.VMEM((PIECE, KV), bf16),
            dma(6),
        ],
        compiler_params=pltpu.CompilerParams(vmem_limit_bytes=16 << 20),
        name="final",
    )(b, o, c)


def solution(mesh):
    in_specs = (P("dp", "rows"), P("dp", None), P("dp", "rows", None), P())
    out_specs = (P("dp", "rows", None), P("rows", None), P(("rows", "dp"), None))
    return jax.shard_map(body, mesh=mesh, in_specs=in_specs, out_specs=out_specs, check_vma=False)
```

```python
import functools
import math

import jax
import jax.numpy as jnp
from jax import lax
from jax.experimental import pallas as pl
from jax.experimental.pallas import tpu as pltpu
from jax.sharding import PartitionSpec as P

D = 8192
KV = 1024
RANK = 128
REPLICAS = 32
NX, NY, NZ = 4, 4, 8
TOK = 2048
ROWS = 1024
BLOCK = ROWS // NX
PIECE = BLOCK // NZ
X_ORDER = (2, 1, 3, 0)
Z_FAR = (4, 3, 5, 2, 6, 1, 7)
Z_NEAR = (1, 7, 2, 6, 3, 5, 4)
DIRECT = (4, 3, 5)
STAGED = (2, 6, 1, 7)
BEFORE_X = (0, 1)
BEFORE_Z = (2, 3)
WINDOW = 6
CUT = 96
f32, bf16 = jnp.float32, jnp.bfloat16
HIGH = lax.Precision.HIGHEST
MESH = pl.DeviceIdType.MESH
TN = (((0,), (0,)), ((), ()))
NT = (((1,), (1,)), ((), ()))


def split(v):
    hi = v.astype(bf16)
    return hi, (v - hi.astype(f32)).astype(bf16)


def dot(a, b, dims=(((1,), (0,)), ((), ()))):
    return lax.dot_general(a, b, dims, preferred_element_type=f32)


def eliminate(a_ref, e_ref, inv_ref, first, last):
    tiles = RANK // 8
    a = {i: a_ref[8 * i : 8 * i + 8] for i in range(first // 8, tiles)}
    e = {i: e_ref[8 * i : 8 * i + 8] for i in range(first // 8, tiles)}
    upper = lax.broadcasted_iota(jnp.int32, (8, 1), 0) >= 4
    for k in range(first, last, 4):
        t, s = divmod(k, 8)
        ra = [a[t][s + j : s + j + 1] for j in range(4)]
        re = [e[t][s + j : s + j + 1] for j in range(4)]
        g = {(i, j): jnp.broadcast_to(ra[i][:, k + j : k + j + 1], (1, RANK)) for i in range(4) for j in range(i, 4)}
        wa, we, low = [None] * 4, [None] * 4, {}
        for j in range(4):
            inv = 1.0 / g[j, j]
            for i in range(j + 1, 4):
                low[i, j] = g[j, i] * inv
                for m in range(i, 4):
                    g[i, m] = g[i, m] - low[i, j] * g[j, m]
            for i in range(j + 1, 4):
                ra[i] = ra[i] - low[i, j] * ra[j]
                re[i] = re[i] - low[i, j] * re[j]
            inv_ref[k + j : k + j + 1] = re[j] / jnp.sqrt(g[j, j])
            wa[j], we[j] = ra[j] * inv, re[j] * inv
        for j in (2, 1, 0):
            for i in range(j + 1, 4):
                wa[j] = wa[j] - low[i, j] * wa[i]
                we[j] = we[j] - low[i, j] * we[i]
        for i in range(t, tiles):
            if i == t and s == 4:
                continue
            m = [a[i][:, k + j : k + j + 1] for j in range(4)]
            if i == t:
                m = [jnp.where(upper, v, 0.0) for v in m]
            a[i] = a[i] - ((m[0] * wa[0] + m[1] * wa[1]) + (m[2] * wa[2] + m[3] * wa[3]))
            e[i] = e[i] - ((m[0] * we[0] + m[1] * we[1]) + (m[2] * we[2] + m[3] * we[3]))
    for i in range(last // 8, tiles):
        a_ref[8 * i : 8 * i + 8] = a[i]
        e_ref[8 * i : 8 * i + 8] = e[i]


def main_kernel(
    acts, kgrads, mom, basis,
    b_v, o_v, c_v,
    a_v, k_v, kq_v, bh_v, bl_v, q_v, p_v, x_in, d_in, z_src, z_in, s_v, s2_v, g_blk, g_mine, g_part, g_y, g_tot, g_rem,
    u_out, u_own, c_in, half, xy_in, v_in, u_all, own_v, ga, ge, inv_v,
    load_sem, send_sem, x_sem, d_sem, z_sem, zag_sem, xag_sem, g_sem, gy_sem, gr_sem, c_sem, xy_sem, v_sem, xyag_sem, cag_sem,
):
    dp = lax.axis_index("dp")
    rows = lax.axis_index("rows")
    x, z = dp // NZ, dp % NZ
    y, core = rows // 2, rows % 2
    sends = []

    def device(xo=0, yo=0, zo=0, flip=False):
        c = 1 - core if flip else core
        return (((x + xo) % NX) * NZ + (z + zo) % NZ, ((y + yo) % NY) * 2 + c)

    def send(src, dst, sem, to):
        copy = pltpu.make_async_remote_copy(
            src_ref=src, dst_ref=dst, send_sem=send_sem.at[len(sends)], recv_sem=sem, device_id=to, device_id_type=MESH
        )
        copy.start()
        sends.append(copy)

    def arrive(dst, sem):
        pltpu.make_async_copy(dst, dst, sem).wait()

    quarter = TOK // 4
    load_q = pltpu.make_async_copy(basis, q_v, load_sem.at[12])
    load_k = [
        pltpu.make_async_copy(kgrads.at[pl.ds(quarter * i, quarter)], k_v.at[pl.ds(quarter * i, quarter)], load_sem.at[8 + i])
        for i in range(4)
    ]
    load_a, load_m = {}, {}
    for o in X_ORDER:
        at = pl.ds(pl.multiple_of(((x + o) % NX) * BLOCK, BLOCK), BLOCK)
        load_a[o] = pltpu.make_async_copy(acts.at[:, at], a_v.at[o], load_sem.at[o])
        load_m[o] = pltpu.make_async_copy(mom.at[0, at], b_v.at[o], load_sem.at[4 + o])
    loads = [load_q] + load_k
    for o in X_ORDER:
        loads += [load_a[o], load_m[o]]
    for copy in loads[:WINDOW]:
        copy.start()
    waiting = iter(loads[WINDOW:])

    def loaded(copy):
        copy.wait()
        for later in waiting:
            later.start()
            break

    barrier = pltpu.get_barrier_semaphore()
    peers = [(xo, yo, 0, False) for xo in range(NX) for yo in range(NY) if (xo, yo) != (0, 0)]
    peers += [(0, 0, zo, False) for zo in range(1, NZ)] + [(0, 0, 0, True)]
    peers += [(xo, 0, zo, False) for xo in range(1, NX) for zo in DIRECT]
    for peer in peers:
        pl.semaphore_signal(barrier, inc=1, device_id=device(*peer), device_id_type=MESH)

    loaded(load_q)
    qh, ql = split(q_v[...])
    q2 = jnp.concatenate([qh, ql], axis=1)
    for i in range(4):
        loaded(load_k[i])
        at = slice(quarter * i, quarter * i + quarter)
        two = dot(k_v[at], q2)
        kq_v[at, :RANK], kq_v[at, RANK:] = split(two[:, :RANK] + two[:, RANK:])
    def slot(zo):
        return (zo + 2) % NZ

    for o in X_ORDER:
        loaded(load_a[o])
        loaded(load_m[o])
        mh, ml = split(b_v[o])
        two = dot(a_v[o], kq_v[...], TN) + dot(mh, q2)
        p = two[:, :RANK] + (two[:, RANK:] + dot(ml, qh))
        for k in range(NZ):
            p_v[o, (k + NZ - z + 2) % NZ] = p[PIECE * k : PIECE * k + PIECE]
        if o == X_ORDER[0]:
            pl.semaphore_wait(barrier, len(peers))
        if o:
            send(p_v.at[o, pl.ds(0, 5)], x_in.at[o - 1], x_sem, device(xo=o))
        for zo in DIRECT:
            send(p_v.at[o, slot(zo)], d_in.at[o, zo - 3], d_sem, device(xo=o, zo=zo))

    def blend(o):
        b = b_v[o] + dot(a_v[o], k_v[...], TN)
        b_v[o] = b
        bh_v[o], bl_v[o] = split(b)

    for o in BEFORE_X:
        blend(o)

    arrive(x_in, x_sem)
    z_src[...] = (p_v[0, :5] + x_in[0]) + (x_in[1] + x_in[2])
    for n, o in enumerate(STAGED):
        send(z_src.at[slot(o)], z_in.at[n], z_sem, device(zo=o))
    for o in BEFORE_Z:
        blend(o)
    mine = z_src[slot(0)]
    arrive(d_in, d_sem)
    for xo in range(NX):
        mine = mine + ((d_in[xo, 0] + d_in[xo, 1]) + d_in[xo, 2])
    arrive(z_in, z_sem)
    mine = mine + ((z_in[0] + z_in[1]) + (z_in[2] + z_in[3]))
    own_v[...] = mine * (1.0 / REPLICAS)
    s_v[0, z] = own_v[...]

    for o in DIRECT:
        for xo in (2, 1, 3, 0):
            sem = xag_sem.at[NX - xo - 1] if xo else zag_sem.at[o - 1]
            send(own_v, s_v.at[(NX - xo) % NX, z], sem, device(xo=xo, zo=o))
        if o == DIRECT[0]:
            for near in STAGED:
                send(own_v, s_v.at[0, z], zag_sem.at[near - 1], device(zo=near))
    for xo in (2, 1, 3):
        send(own_v, s_v.at[NX - xo, z], xag_sem.at[NX - xo - 1], device(xo=xo))
    for o in Z_NEAR:
        at = (z + NZ - o) % NZ
        arrive(s_v.at[0, at], zag_sem.at[o - 1])
        if o in STAGED:
            for xo in (2, 1, 3):
                send(s_v.at[0, at], s_v.at[NX - xo, at], xag_sem.at[NX - xo - 1], device(xo=xo))

    def gram(o):
        s = s_v[o].reshape(BLOCK, RANK)
        g_blk[(x + o) % NX] = lax.dot_general(s, s, TN, precision=HIGH, preferred_element_type=f32)

    def halves(o):
        s2_v[o, :, :RANK], s2_v[o, :, RANK:] = split(s_v[o].reshape(BLOCK, RANK))

    gram(0)
    for o in (0, 1, 3, 2):
        if o:
            arrive(s_v.at[o], xag_sem.at[o - 1])
        halves(o)

    def right(dst, which):
        cols = pl.ds(pl.multiple_of(512 * which, 512), 512)
        s2 = s2_v[...].reshape(ROWS, 2 * RANK)
        big = dot(s2, bh_v[:, :, cols].reshape(ROWS, 512), TN)
        small = dot(s2[:, :RANK], bl_v[:, :, cols].reshape(ROWS, 512), TN)
        u = big[:RANK] + (big[RANK:] + small)
        for b in range(4):
            dst[b] = u[:, 128 * b : 128 * b + 128]

    right(u_out, 1 - core)
    for xo in (2, 1, 3, 0):
        to_x = (x + xo) % NX
        send(u_out.at[to_x], c_in.at[to_x], c_sem.at[xo], device(flip=True))
    for o in (1, 3, 2):
        gram(o)
    mine_at = pl.ds(pl.multiple_of(64 * core, 64), 64)
    other_at = pl.ds(pl.multiple_of(64 * (1 - core), 64), 64)
    g_mine[...] = (g_blk[0] + g_blk[1]) + (g_blk[2] + g_blk[3])
    send(g_mine.at[other_at], g_part, g_sem, device(flip=True))
    right(u_own, core)
    for xo in (2, 1, 3, 0):
        to_x = (x + xo) % NX
        arrive(c_in.at[to_x], c_sem.at[xo])
        tot = u_own[to_x] + c_in[to_x]
        for r in range(4):
            half[to_x, r] = tot[32 * r : 32 * r + 32]
        for yo in (2, 1, 3, 0):
            if (xo, yo) != (0, 0):
                send(half.at[to_x, (y + yo) % NY], xy_in.at[xo * NY + yo - 1], xy_sem, device(xo=xo, yo=yo))
    arrive(g_part, g_sem)
    g_y[y] = g_mine[mine_at] + g_part[...]
    for yo in (2, 1, 3):
        send(g_y.at[y], g_y.at[y], gy_sem.at[yo - 1], device(yo=yo))
    me = x * NY + y
    for yo in (1, 3, 2):
        arrive(g_y.at[(y + NY - yo) % NY], gy_sem.at[yo - 1])
    g_tot[...] = (g_y[0] + g_y[1]) + (g_y[2] + g_y[3])
    send(g_tot, g_rem, gr_sem, device(flip=True))
    tot = half[x, y]
    arrive(xy_in, xy_sem)
    for o in range(NX * NY - 1):
        tot = tot + xy_in[o]
    v_in[z] = tot
    for o in Z_FAR:
        send(v_in.at[z], v_in.at[z], v_sem.at[o - 1], device(zo=o))
    arrive(g_rem, gr_sem)
    ga[mine_at] = g_tot[...]
    ga[other_at] = g_rem[...]
    eye = lax.broadcasted_iota(jnp.int32, (RANK, RANK), 0) == lax.broadcasted_iota(jnp.int32, (RANK, RANK), 1)
    ge[...] = eye.astype(f32)
    eliminate(ga, ge, inv_v, 0, CUT)
    for o in Z_NEAR:
        arrive(v_in.at[(z + NZ - o) % NZ], v_sem.at[o - 1])
    tot = v_in[0]
    for o in range(1, NZ):
        tot = tot + v_in[o]
    u_all[core, me] = tot
    order = sorted(
        ((xo, yo) for xo in range(NX) for yo in range(NY) if (xo, yo) != (0, 0)),
        key=lambda o: -min(o[0], NX - o[0]) - min(o[1], NY - o[1]),
    )
    for xo, yo in order:
        send(u_all.at[core, me], u_all.at[core, me], xyag_sem.at[xo * NY + yo - 1], device(xo=xo, yo=yo))
    send(u_all.at[core, me], u_all.at[core, me], cag_sem, device(flip=True))
    eliminate(ga, ge, inv_v, CUT, RANK)
    inverse = inv_v[...]
    for o in range(NX):
        o_v[o] = lax.dot_general(s_v[o].reshape(BLOCK, RANK), inverse, NT, precision=HIGH, preferred_element_type=f32)
    for xo, yo in reversed(order):
        at = ((x + NX - xo) % NX) * NY + (y + NY - yo) % NY
        arrive(u_all.at[core, at], xyag_sem.at[xo * NY + yo - 1])
        send(u_all.at[core, at], u_all.at[core, at], cag_sem, device(flip=True))

    def finish(which):
        for b in range(4):
            ut = u_all[which, pl.ds(4 * b, 4)].reshape(RANK, 128)
            c_v[4 * which + b] = jnp.dot(inverse, ut, precision=HIGH, preferred_element_type=f32) * (1.0 / REPLICAS)

    finish(core)
    arrive(u_all.at[1 - core], cag_sem)
    finish(1 - core)
    for copy in sends:
        copy.wait_send()


def final_kernel(b_ref, o_ref, c_ref, new_ref, basis_ref, upd_ref, c2_v, cl_v, n_v, new_v, basis_v, upd_v, sem):
    x, z = lax.axis_index("dp") // NZ, lax.axis_index("dp") % NZ
    squares = 0.0
    for b in range(8):
        cols = slice(128 * b, 128 * b + 128)
        v = c_ref[b]
        ch, cl_v[:, cols] = split(v)
        c2_v[:RANK, cols] = ch
        c2_v[RANK:, cols] = ch
        squares = squares + v * v
    copies = []
    for o in range(NX):
        oh, ol = split(o_ref[o])
        feedback = dot(jnp.concatenate([oh, ol], axis=1), c2_v[...]) + dot(oh, cl_v[...])
        new_v[o] = b_ref[o] - 0.2 * feedback
        at = pl.ds(pl.multiple_of(((x + o) % NX) * BLOCK, BLOCK), BLOCK)
        copies.append(pltpu.make_async_copy(new_v.at[o], new_ref.at[0, at], sem.at[o]))
        copies[-1].start()
        if o == 0:
            norm = jnp.sqrt(jnp.sum(squares, axis=1, keepdims=True) + 1e-06)
            own_h, own_l = split(o_ref[0, pl.ds(pl.multiple_of(z * PIECE, PIECE), PIECE)])
            for b in range(8):
                n_v[b] = c_ref[b] / norm
                nh, nl = split(n_v[b])
                upd = dot(own_h, nh) + (dot(own_h, nl) + dot(own_l, nh))
                upd_v[:, 128 * b : 128 * b + 128] = (math.sqrt(D * KV / RANK) * upd).astype(bf16)
            basis_v[...] = n_v[lax.axis_index("rows")].T
            copies.append(pltpu.make_async_copy(upd_v, upd_ref, sem.at[4]))
            copies[-1].start()
            copies.append(pltpu.make_async_copy(basis_v, basis_ref, sem.at[5]))
            copies[-1].start()
    for copy in copies:
        copy.wait()


def body(activations, key_grads, momentum, basis):
    hbm = pl.BlockSpec(memory_space=pl.ANY)
    vmem = pl.BlockSpec(memory_space=pltpu.VMEM)
    sds = jax.ShapeDtypeStruct
    dma = lambda *n: pltpu.SemaphoreType.DMA(n)
    one = pltpu.SemaphoreType.DMA
    b, o, c = pl.pallas_call(
        main_kernel,
        out_shape=(sds((NX, BLOCK, KV), f32), sds((NX, BLOCK, RANK), f32), sds((8, RANK, 128), f32)),
        in_specs=[pl.BlockSpec(memory_space=pltpu.HBM)] * 4,
        out_specs=(vmem,) * 3,
        scratch_shapes=[
            pltpu.VMEM((NX, TOK, BLOCK), bf16),
            pltpu.VMEM((TOK, KV), bf16),
            pltpu.VMEM((TOK, 2 * RANK), bf16),
            pltpu.VMEM((NX, BLOCK, KV), bf16),
            pltpu.VMEM((NX, BLOCK, KV), bf16),
            pltpu.VMEM((KV, RANK), f32),
            pltpu.VMEM((NX, NZ, PIECE, RANK), f32),
            pltpu.VMEM((NX - 1, 5, PIECE, RANK), f32),
            pltpu.VMEM((NX, 3, PIECE, RANK), f32),
            pltpu.VMEM((5, PIECE, RANK), f32),
            pltpu.VMEM((4, PIECE, RANK), f32),
            pltpu.VMEM((NX, NZ, PIECE, RANK), f32),
            pltpu.VMEM((NX, BLOCK, 2 * RANK), bf16),
            pltpu.VMEM((NX, RANK, RANK), f32),
            pltpu.VMEM((RANK, RANK), f32),
            pltpu.VMEM((64, RANK), f32),
            pltpu.VMEM((NY, 64, RANK), f32),
            pltpu.VMEM((64, RANK), f32),
            pltpu.VMEM((64, RANK), f32),
            pltpu.VMEM((4, RANK, 128), f32),
            pltpu.VMEM((4, RANK, 128), f32),
            pltpu.VMEM((4, RANK, 128), f32),
            pltpu.VMEM((NX, NY, 32, 128), f32),
            pltpu.VMEM((15, 32, 128), f32),
            pltpu.VMEM((NZ, 32, 128), f32),
            pltpu.VMEM((2, 16, 32, 128), f32),
            pltpu.VMEM((PIECE, RANK), f32),
            pltpu.VMEM((RANK, RANK), f32),
            pltpu.VMEM((RANK, RANK), f32),
            pltpu.VMEM((RANK, RANK), f32),
            dma(13), dma(136), one, one, one, dma(7), dma(3), one, dma(3), one, dma(4), one, dma(7), dma(15), one,
        ],
        compiler_params=pltpu.CompilerParams(collective_id=0, has_side_effects=True, vmem_limit_bytes=36 << 20),
        name="main",
    )(*(pltpu.with_memory_space_constraint(v, pltpu.HBM) for v in (activations, key_grads, momentum, basis)))
    return pl.pallas_call(
        final_kernel,
        out_shape=(sds((1, ROWS, KV), f32), sds((RANK, RANK), f32), sds((PIECE, KV), bf16)),
        in_specs=[vmem] * 3,
        out_specs=(hbm,) * 3,
        scratch_shapes=[
            pltpu.VMEM((2 * RANK, KV), bf16),
            pltpu.VMEM((RANK, KV), bf16),
            pltpu.VMEM((8, RANK, 128), f32),
            pltpu.VMEM((NX, BLOCK, KV), f32),
            pltpu.VMEM((RANK, RANK), f32),
            pltpu.VMEM((PIECE, KV), bf16),
            dma(6),
        ],
        compiler_params=pltpu.CompilerParams(vmem_limit_bytes=16 << 20),
        name="final",
    )(b, o, c)


def solution(mesh):
    in_specs = (P("dp", "rows"), P("dp", None), P("dp", "rows", None), P())
    out_specs = (P("dp", "rows", None), P("rows", None), P(("rows", "dp"), None))
    return jax.shard_map(body, mesh=mesh, in_specs=in_specs, out_specs=out_specs, check_vma=False)
```

```python
import functools
import math

import jax
import jax.numpy as jnp
from jax import lax
from jax.experimental import pallas as pl
from jax.experimental.pallas import tpu as pltpu
from jax.sharding import PartitionSpec as P

D = 8192
KV = 1024
RANK = 128
REPLICAS = 32
NX, NY, NZ = 4, 4, 8
TOK = 2048
ROWS = 1024
BLOCK = ROWS // NX
PIECE = BLOCK // NZ
X_ORDER = (2, 1, 3, 0)
Z_FAR = (4, 3, 5, 2, 6, 1, 7)
Z_NEAR = (1, 7, 2, 6, 3, 5, 4)
RS_DIRECT = (4, 3, 5)
AG_DIRECT = ()
RS_STAGED = tuple(o for o in Z_FAR if o not in RS_DIRECT)
AG_STAGED = tuple(o for o in Z_FAR if o not in AG_DIRECT)
KEPT = NZ - len(RS_DIRECT)
BEFORE_X = (0, 1)
BEFORE_Z = (2, 3)
WINDOW = 6
CUT = 56
f32, bf16 = jnp.float32, jnp.bfloat16
HIGH = lax.Precision.HIGHEST
MESH = pl.DeviceIdType.MESH
TN = (((0,), (0,)), ((), ()))
NT = (((1,), (1,)), ((), ()))


def split(v):
    hi = v.astype(bf16)
    return hi, (v - hi.astype(f32)).astype(bf16)


def dot(a, b, dims=(((1,), (0,)), ((), ()))):
    return lax.dot_general(a, b, dims, preferred_element_type=f32)


def eliminate(a_ref, e_ref, inv_ref, first, last):
    tiles = RANK // 8
    a = {i: a_ref[8 * i : 8 * i + 8] for i in range(first // 8, tiles)}
    e = {i: e_ref[8 * i : 8 * i + 8] for i in range(first // 8, tiles)}
    upper = lax.broadcasted_iota(jnp.int32, (8, 1), 0) >= 4
    for k in range(first, last, 4):
        t, s = divmod(k, 8)
        ra = [a[t][s + j : s + j + 1] for j in range(4)]
        re = [e[t][s + j : s + j + 1] for j in range(4)]
        g = {(i, j): jnp.broadcast_to(ra[i][:, k + j : k + j + 1], (1, RANK)) for i in range(4) for j in range(i, 4)}
        wa, we, low = [None] * 4, [None] * 4, {}
        for j in range(4):
            inv = 1.0 / g[j, j]
            for i in range(j + 1, 4):
                low[i, j] = g[j, i] * inv
                for m in range(i, 4):
                    g[i, m] = g[i, m] - low[i, j] * g[j, m]
            for i in range(j + 1, 4):
                ra[i] = ra[i] - low[i, j] * ra[j]
                re[i] = re[i] - low[i, j] * re[j]
            inv_ref[k + j : k + j + 1] = re[j] / jnp.sqrt(g[j, j])
            wa[j], we[j] = ra[j] * inv, re[j] * inv
        for j in (2, 1, 0):
            for i in range(j + 1, 4):
                wa[j] = wa[j] - low[i, j] * wa[i]
                we[j] = we[j] - low[i, j] * we[i]
        for i in range(t, tiles):
            if i == t and s == 4:
                continue
            m = [a[i][:, k + j : k + j + 1] for j in range(4)]
            if i == t:
                m = [jnp.where(upper, v, 0.0) for v in m]
            a[i] = a[i] - ((m[0] * wa[0] + m[1] * wa[1]) + (m[2] * wa[2] + m[3] * wa[3]))
            e[i] = e[i] - ((m[0] * we[0] + m[1] * we[1]) + (m[2] * we[2] + m[3] * we[3]))
    for i in range(last // 8, tiles):
        a_ref[8 * i : 8 * i + 8] = a[i]
        e_ref[8 * i : 8 * i + 8] = e[i]


def main_kernel(
    acts, kgrads, mom, basis,
    b_v, o_v, c_v,
    a_v, k_v, kq_v, bh_v, bl_v, q_v, p_v, x_in, d_in, z_src, z_in, s_v, s2_v, g_blk, g_mine, g_part, g_y, g_tot, g_rem,
    u_out, u_own, c_in, half, xy_in, v_in, u_all, own_v, ga, ge, inv_v,
    load_sem, send_sem, x_sem, d_sem, z_sem, zag_sem, xag_sem, g_sem, gy_sem, gr_sem, c_sem, xy_sem, v_sem, xyag_sem, cag_sem,
):
    dp = lax.axis_index("dp")
    rows = lax.axis_index("rows")
    x, z = dp // NZ, dp % NZ
    y, core = rows // 2, rows % 2
    sends = []

    def device(xo=0, yo=0, zo=0, flip=False):
        c = 1 - core if flip else core
        return (((x + xo) % NX) * NZ + (z + zo) % NZ, ((y + yo) % NY) * 2 + c)

    def send(src, dst, sem, to):
        copy = pltpu.make_async_remote_copy(
            src_ref=src, dst_ref=dst, send_sem=send_sem.at[len(sends)], recv_sem=sem, device_id=to, device_id_type=MESH
        )
        copy.start()
        sends.append(copy)

    def arrive(dst, sem):
        pltpu.make_async_copy(dst, dst, sem).wait()

    quarter = TOK // 4
    load_q = pltpu.make_async_copy(basis, q_v, load_sem.at[12])
    load_k = [
        pltpu.make_async_copy(kgrads.at[pl.ds(quarter * i, quarter)], k_v.at[pl.ds(quarter * i, quarter)], load_sem.at[8 + i])
        for i in range(4)
    ]
    load_a, load_m = {}, {}
    for o in X_ORDER:
        at = pl.ds(pl.multiple_of(((x + o) % NX) * BLOCK, BLOCK), BLOCK)
        load_a[o] = pltpu.make_async_copy(acts.at[:, at], a_v.at[o], load_sem.at[o])
        load_m[o] = pltpu.make_async_copy(mom.at[0, at], b_v.at[o], load_sem.at[4 + o])
    loads = [load_q] + load_k
    for o in X_ORDER:
        loads += [load_a[o], load_m[o]]
    for copy in loads[:WINDOW]:
        copy.start()
    waiting = iter(loads[WINDOW:])

    def loaded(copy):
        copy.wait()
        for later in waiting:
            later.start()
            break

    barrier = pltpu.get_barrier_semaphore()
    peers = [(xo, yo, 0, False) for xo in range(NX) for yo in range(NY) if (xo, yo) != (0, 0)]
    peers += [(0, 0, zo, False) for zo in range(1, NZ)] + [(0, 0, 0, True)]
    peers += [(xo, 0, zo, False) for xo in range(1, NX) for zo in sorted(RS_DIRECT + AG_DIRECT)]
    for peer in peers:
        pl.semaphore_signal(barrier, inc=1, device_id=device(*peer), device_id_type=MESH)

    loaded(load_q)
    qh, ql = split(q_v[...])
    q2 = jnp.concatenate([qh, ql], axis=1)
    for i in range(4):
        loaded(load_k[i])
        at = slice(quarter * i, quarter * i + quarter)
        two = dot(k_v[at], q2)
        kq_v[at, :RANK], kq_v[at, RANK:] = split(two[:, :RANK] + two[:, RANK:])
    def slot(zo):
        return (zo + (KEPT - 1) // 2) % NZ

    for o in X_ORDER:
        loaded(load_a[o])
        loaded(load_m[o])
        mh, ml = split(b_v[o])
        two = dot(a_v[o], kq_v[...], TN) + dot(mh, q2)
        p = two[:, :RANK] + (two[:, RANK:] + dot(ml, qh))
        for k in range(NZ):
            p_v[o, slot(k + NZ - z)] = p[PIECE * k : PIECE * k + PIECE]
        if o == X_ORDER[0]:
            pl.semaphore_wait(barrier, len(peers))
        if o:
            send(p_v.at[o, pl.ds(0, KEPT)], x_in.at[o - 1], x_sem, device(xo=o))
        for n, zo in enumerate(RS_DIRECT):
            send(p_v.at[o, slot(zo)], d_in.at[o, n], d_sem, device(xo=o, zo=zo))

    def blend(o):
        b = b_v[o] + dot(a_v[o], k_v[...], TN)
        b_v[o] = b
        bh_v[o], bl_v[o] = split(b)

    for o in BEFORE_X:
        blend(o)

    arrive(x_in, x_sem)
    z_src[...] = (p_v[0, :KEPT] + x_in[0]) + (x_in[1] + x_in[2])
    for n, o in enumerate(RS_STAGED):
        send(z_src.at[slot(o)], z_in.at[n], z_sem, device(zo=o))
    for o in BEFORE_Z:
        blend(o)
    mine = z_src[slot(0)]
    if RS_DIRECT:
        arrive(d_in, d_sem)
        for xo in range(NX):
            for n in range(len(RS_DIRECT)):
                mine = mine + d_in[xo, n]
    arrive(z_in, z_sem)
    for n in range(KEPT - 1):
        mine = mine + z_in[n]
    own_v[...] = mine * (1.0 / REPLICAS)
    s_v[0, z] = own_v[...]

    for o in Z_FAR:
        send(own_v, s_v.at[0, z], zag_sem.at[o - 1], device(zo=o))
        if o in AG_DIRECT:
            for xo in (2, 1, 3):
                send(own_v, s_v.at[NX - xo, z], xag_sem.at[NX - xo - 1], device(xo=xo, zo=o))
    for xo in (2, 1, 3):
        send(own_v, s_v.at[NX - xo, z], xag_sem.at[NX - xo - 1], device(xo=xo))
    for o in Z_NEAR:
        at = (z + NZ - o) % NZ
        arrive(s_v.at[0, at], zag_sem.at[o - 1])
        if o in AG_STAGED:
            for xo in (2, 1, 3):
                send(s_v.at[0, at], s_v.at[NX - xo, at], xag_sem.at[NX - xo - 1], device(xo=xo))

    def gram(o):
        s = s_v[o].reshape(BLOCK, RANK)
        g_blk[(x + o) % NX] = lax.dot_general(s, s, TN, precision=HIGH, preferred_element_type=f32)

    def halves(o):
        s2_v[o, :, :RANK], s2_v[o, :, RANK:] = split(s_v[o].reshape(BLOCK, RANK))

    gram(0)
    for o in (0, 1, 3, 2):
        if o:
            arrive(s_v.at[o], xag_sem.at[o - 1])
        halves(o)

    def right(dst, which):
        cols = pl.ds(pl.multiple_of(512 * which, 512), 512)
        s2 = s2_v[...].reshape(ROWS, 2 * RANK)
        big = dot(s2, bh_v[:, :, cols].reshape(ROWS, 512), TN)
        small = dot(s2[:, :RANK], bl_v[:, :, cols].reshape(ROWS, 512), TN)
        u = big[:RANK] + (big[RANK:] + small)
        for b in range(4):
            dst[b] = u[:, 128 * b : 128 * b + 128]

    right(u_out, 1 - core)
    for xo in (2, 1, 3, 0):
        to_x = (x + xo) % NX
        send(u_out.at[to_x], c_in.at[to_x], c_sem.at[xo], device(flip=True))
    for o in (1, 3, 2):
        gram(o)
    mine_at = pl.ds(pl.multiple_of(64 * core, 64), 64)
    other_at = pl.ds(pl.multiple_of(64 * (1 - core), 64), 64)
    g_mine[...] = (g_blk[0] + g_blk[1]) + (g_blk[2] + g_blk[3])
    send(g_mine.at[other_at], g_part, g_sem, device(flip=True))
    right(u_own, core)
    for xo in (2, 1, 3, 0):
        to_x = (x + xo) % NX
        arrive(c_in.at[to_x], c_sem.at[xo])
        tot = u_own[to_x] + c_in[to_x]
        for r in range(4):
            half[to_x, r] = tot[32 * r : 32 * r + 32]
        for yo in (2, 1, 3, 0):
            if (xo, yo) != (0, 0):
                send(half.at[to_x, (y + yo) % NY], xy_in.at[xo * NY + yo - 1], xy_sem, device(xo=xo, yo=yo))
    arrive(g_part, g_sem)
    g_y[y] = g_mine[mine_at] + g_part[...]
    for yo in (2, 1, 3):
        send(g_y.at[y], g_y.at[y], gy_sem.at[yo - 1], device(yo=yo))
    me = x * NY + y
    tot = half[x, y]
    arrive(xy_in, xy_sem)
    for o in range(NX * NY - 1):
        tot = tot + xy_in[o]
    v_in[z] = tot
    for o in Z_FAR:
        send(v_in.at[z], v_in.at[z], v_sem.at[o - 1], device(zo=o))
    for yo in (1, 3, 2):
        arrive(g_y.at[(y + NY - yo) % NY], gy_sem.at[yo - 1])
    g_tot[...] = (g_y[0] + g_y[1]) + (g_y[2] + g_y[3])
    send(g_tot, g_rem, gr_sem, device(flip=True))
    ga[mine_at] = g_tot[...]
    arrive(g_rem, gr_sem)
    ga[other_at] = g_rem[...]
    eye = lax.broadcasted_iota(jnp.int32, (RANK, RANK), 0) == lax.broadcasted_iota(jnp.int32, (RANK, RANK), 1)
    ge[...] = eye.astype(f32)
    eliminate(ga, ge, inv_v, 0, CUT)
    for o in Z_NEAR:
        arrive(v_in.at[(z + NZ - o) % NZ], v_sem.at[o - 1])
    tot = v_in[0]
    for o in range(1, NZ):
        tot = tot + v_in[o]
    u_all[core, me] = tot
    order = sorted(
        ((xo, yo) for xo in range(NX) for yo in range(NY) if (xo, yo) != (0, 0)),
        key=lambda o: -min(o[0], NX - o[0]) - min(o[1], NY - o[1]),
    )
    for xo, yo in order:
        send(u_all.at[core, me], u_all.at[core, me], xyag_sem.at[xo * NY + yo - 1], device(xo=xo, yo=yo))
    send(u_all.at[core, me], u_all.at[core, me], cag_sem, device(flip=True))
    eliminate(ga, ge, inv_v, CUT, RANK)
    inverse = inv_v[...]
    for o in range(NX):
        o_v[o] = lax.dot_general(s_v[o].reshape(BLOCK, RANK), inverse, NT, precision=HIGH, preferred_element_type=f32)
    for xo, yo in reversed(order):
        at = ((x + NX - xo) % NX) * NY + (y + NY - yo) % NY
        arrive(u_all.at[core, at], xyag_sem.at[xo * NY + yo - 1])
        send(u_all.at[core, at], u_all.at[core, at], cag_sem, device(flip=True))

    def finish(which):
        for b in range(4):
            ut = u_all[which, pl.ds(4 * b, 4)].reshape(RANK, 128)
            c_v[4 * which + b] = jnp.dot(inverse, ut, precision=HIGH, preferred_element_type=f32) * (1.0 / REPLICAS)

    finish(core)
    arrive(u_all.at[1 - core], cag_sem)
    finish(1 - core)
    for copy in sends:
        copy.wait_send()


def final_kernel(b_ref, o_ref, c_ref, new_ref, basis_ref, upd_ref, c2_v, cl_v, n_v, new_v, basis_v, upd_v, sem):
    x, z = lax.axis_index("dp") // NZ, lax.axis_index("dp") % NZ
    squares = 0.0
    for b in range(8):
        cols = slice(128 * b, 128 * b + 128)
        v = c_ref[b]
        ch, cl_v[:, cols] = split(v)
        c2_v[:RANK, cols] = ch
        c2_v[RANK:, cols] = ch
        squares = squares + v * v
    copies = []
    for o in range(NX):
        oh, ol = split(o_ref[o])
        feedback = dot(jnp.concatenate([oh, ol], axis=1), c2_v[...]) + dot(oh, cl_v[...])
        new_v[o] = b_ref[o] - 0.2 * feedback
        at = pl.ds(pl.multiple_of(((x + o) % NX) * BLOCK, BLOCK), BLOCK)
        copies.append(pltpu.make_async_copy(new_v.at[o], new_ref.at[0, at], sem.at[o]))
        copies[-1].start()
        if o == 0:
            norm = jnp.sqrt(jnp.sum(squares, axis=1, keepdims=True) + 1e-06)
            own_h, own_l = split(o_ref[0, pl.ds(pl.multiple_of(z * PIECE, PIECE), PIECE)])
            for b in range(8):
                n_v[b] = c_ref[b] / norm
                nh, nl = split(n_v[b])
                upd = dot(own_h, nh) + (dot(own_h, nl) + dot(own_l, nh))
                upd_v[:, 128 * b : 128 * b + 128] = (math.sqrt(D * KV / RANK) * upd).astype(bf16)
            basis_v[...] = n_v[lax.axis_index("rows")].T
            copies.append(pltpu.make_async_copy(upd_v, upd_ref, sem.at[4]))
            copies[-1].start()
            copies.append(pltpu.make_async_copy(basis_v, basis_ref, sem.at[5]))
            copies[-1].start()
    for copy in copies:
        copy.wait()


def body(activations, key_grads, momentum, basis):
    hbm = pl.BlockSpec(memory_space=pl.ANY)
    vmem = pl.BlockSpec(memory_space=pltpu.VMEM)
    sds = jax.ShapeDtypeStruct
    dma = lambda *n: pltpu.SemaphoreType.DMA(n)
    one = pltpu.SemaphoreType.DMA
    b, o, c = pl.pallas_call(
        main_kernel,
        out_shape=(sds((NX, BLOCK, KV), f32), sds((NX, BLOCK, RANK), f32), sds((8, RANK, 128), f32)),
        in_specs=[pl.BlockSpec(memory_space=pltpu.HBM)] * 4,
        out_specs=(vmem,) * 3,
        scratch_shapes=[
            pltpu.VMEM((NX, TOK, BLOCK), bf16),
            pltpu.VMEM((TOK, KV), bf16),
            pltpu.VMEM((TOK, 2 * RANK), bf16),
            pltpu.VMEM((NX, BLOCK, KV), bf16),
            pltpu.VMEM((NX, BLOCK, KV), bf16),
            pltpu.VMEM((KV, RANK), f32),
            pltpu.VMEM((NX, NZ, PIECE, RANK), f32),
            pltpu.VMEM((NX - 1, KEPT, PIECE, RANK), f32),
            pltpu.VMEM((NX, max(1, len(RS_DIRECT)), PIECE, RANK), f32),
            pltpu.VMEM((KEPT, PIECE, RANK), f32),
            pltpu.VMEM((KEPT - 1, PIECE, RANK), f32),
            pltpu.VMEM((NX, NZ, PIECE, RANK), f32),
            pltpu.VMEM((NX, BLOCK, 2 * RANK), bf16),
            pltpu.VMEM((NX, RANK, RANK), f32),
            pltpu.VMEM((RANK, RANK), f32),
            pltpu.VMEM((64, RANK), f32),
            pltpu.VMEM((NY, 64, RANK), f32),
            pltpu.VMEM((64, RANK), f32),
            pltpu.VMEM((64, RANK), f32),
            pltpu.VMEM((4, RANK, 128), f32),
            pltpu.VMEM((4, RANK, 128), f32),
            pltpu.VMEM((4, RANK, 128), f32),
            pltpu.VMEM((NX, NY, 32, 128), f32),
            pltpu.VMEM((15, 32, 128), f32),
            pltpu.VMEM((NZ, 32, 128), f32),
            pltpu.VMEM((2, 16, 32, 128), f32),
            pltpu.VMEM((PIECE, RANK), f32),
            pltpu.VMEM((RANK, RANK), f32),
            pltpu.VMEM((RANK, RANK), f32),
            pltpu.VMEM((RANK, RANK), f32),
            dma(13), dma(136), one, one, one, dma(7), dma(3), one, dma(3), one, dma(4), one, dma(7), dma(15), one,
        ],
        compiler_params=pltpu.CompilerParams(collective_id=0, has_side_effects=True, vmem_limit_bytes=36 << 20),
        name="main",
    )(*(pltpu.with_memory_space_constraint(v, pltpu.HBM) for v in (activations, key_grads, momentum, basis)))
    return pl.pallas_call(
        final_kernel,
        out_shape=(sds((1, ROWS, KV), f32), sds((RANK, RANK), f32), sds((PIECE, KV), bf16)),
        in_specs=[vmem] * 3,
        out_specs=(hbm,) * 3,
        scratch_shapes=[
            pltpu.VMEM((2 * RANK, KV), bf16),
            pltpu.VMEM((RANK, KV), bf16),
            pltpu.VMEM((8, RANK, 128), f32),
            pltpu.VMEM((NX, BLOCK, KV), f32),
            pltpu.VMEM((RANK, RANK), f32),
            pltpu.VMEM((PIECE, KV), bf16),
            dma(6),
        ],
        compiler_params=pltpu.CompilerParams(vmem_limit_bytes=16 << 20),
        name="final",
    )(b, o, c)


def solution(mesh):
    in_specs = (P("dp", "rows"), P("dp", None), P("dp", "rows", None), P())
    out_specs = (P("dp", "rows", None), P("rows", None), P(("rows", "dp"), None))
    return jax.shard_map(body, mesh=mesh, in_specs=in_specs, out_specs=out_specs, check_vma=False)
```

```python
import functools
import math

import jax
import jax.numpy as jnp
from jax import lax
from jax.experimental import pallas as pl
from jax.experimental.pallas import tpu as pltpu
from jax.sharding import PartitionSpec as P

D = 8192
KV = 1024
RANK = 128
REPLICAS = 32
NX, NY, NZ = 4, 4, 8
TOK = 2048
ROWS = 1024
BLOCK = ROWS // NX
PIECE = BLOCK // NZ
X_ORDER = (2, 1, 3, 0)
Z_FAR = (4, 3, 5, 2, 6, 1, 7)
Z_NEAR = (1, 7, 2, 6, 3, 5, 4)
RS_DIRECT = (4, 3, 5)
AG_DIRECT = ()
RS_STAGED = tuple(o for o in Z_FAR if o not in RS_DIRECT)
AG_STAGED = tuple(o for o in Z_FAR if o not in AG_DIRECT)
KEPT = NZ - len(RS_DIRECT)
BEFORE_X = (0, 1, 2, 3)
BEFORE_Z = ()
STORED = 128
WINDOW = 6
CUT = 56
f32, bf16 = jnp.float32, jnp.bfloat16
HIGH = lax.Precision.HIGHEST
MESH = pl.DeviceIdType.MESH
TN = (((0,), (0,)), ((), ()))
NT = (((1,), (1,)), ((), ()))


def split(v):
    hi = v.astype(bf16)
    return hi, (v - hi.astype(f32)).astype(bf16)


def dot(a, b, dims=(((1,), (0,)), ((), ()))):
    return lax.dot_general(a, b, dims, preferred_element_type=f32)


def eliminate(a_ref, e_ref, inv_ref, first, last):
    tiles = RANK // 8
    a = {i: a_ref[8 * i : 8 * i + 8] for i in range(first // 8, tiles)}
    e = {i: e_ref[8 * i : 8 * i + 8] for i in range(first // 8, tiles)}
    upper = lax.broadcasted_iota(jnp.int32, (8, 1), 0) >= 4
    for k in range(first, last, 4):
        t, s = divmod(k, 8)
        ra = [a[t][s + j : s + j + 1] for j in range(4)]
        re = [e[t][s + j : s + j + 1] for j in range(4)]
        g = {(i, j): jnp.broadcast_to(ra[i][:, k + j : k + j + 1], (1, RANK)) for i in range(4) for j in range(i, 4)}
        wa, we, low = [None] * 4, [None] * 4, {}
        for j in range(4):
            inv = 1.0 / g[j, j]
            for i in range(j + 1, 4):
                low[i, j] = g[j, i] * inv
                for m in range(i, 4):
                    g[i, m] = g[i, m] - low[i, j] * g[j, m]
            for i in range(j + 1, 4):
                ra[i] = ra[i] - low[i, j] * ra[j]
                re[i] = re[i] - low[i, j] * re[j]
            inv_ref[k + j : k + j + 1] = re[j] / jnp.sqrt(g[j, j])
            wa[j], we[j] = ra[j] * inv, re[j] * inv
        for j in (2, 1, 0):
            for i in range(j + 1, 4):
                wa[j] = wa[j] - low[i, j] * wa[i]
                we[j] = we[j] - low[i, j] * we[i]
        for i in range(t, tiles):
            if i == t and s == 4:
                continue
            m = [a[i][:, k + j : k + j + 1] for j in range(4)]
            if i == t:
                m = [jnp.where(upper, v, 0.0) for v in m]
            a[i] = a[i] - ((m[0] * wa[0] + m[1] * wa[1]) + (m[2] * wa[2] + m[3] * wa[3]))
            e[i] = e[i] - ((m[0] * we[0] + m[1] * we[1]) + (m[2] * we[2] + m[3] * we[3]))
    for i in range(last // 8, tiles):
        a_ref[8 * i : 8 * i + 8] = a[i]
        e_ref[8 * i : 8 * i + 8] = e[i]


def main_kernel(
    acts, kgrads, mom, basis,
    b_v, o_v, c_v,
    a_v, k_v, kq_v, bh_v, bl_v, q_v, p_v, x_in, d_in, z_src, z_in, s_v, s2_v, g_blk, g_mine, g_part, g_y, g_tot, g_rem,
    u_out, u_own, c_in, half, xy_in, v_in, u_all, own_v, ga, ge, inv_v,
    load_sem, send_sem, x_sem, d_sem, z_sem, zag_sem, xag_sem, g_sem, gy_sem, gr_sem, c_sem, xy_sem, v_sem, xyag_sem, cag_sem,
):
    dp = lax.axis_index("dp")
    rows = lax.axis_index("rows")
    x, z = dp // NZ, dp % NZ
    y, core = rows // 2, rows % 2
    sends = []

    def device(xo=0, yo=0, zo=0, flip=False):
        c = 1 - core if flip else core
        return (((x + xo) % NX) * NZ + (z + zo) % NZ, ((y + yo) % NY) * 2 + c)

    def send(src, dst, sem, to):
        copy = pltpu.make_async_remote_copy(
            src_ref=src, dst_ref=dst, send_sem=send_sem.at[len(sends)], recv_sem=sem, device_id=to, device_id_type=MESH
        )
        copy.start()
        sends.append(copy)

    def arrive(dst, sem):
        pltpu.make_async_copy(dst, dst, sem).wait()

    quarter = TOK // 4
    load_q = pltpu.make_async_copy(basis, q_v, load_sem.at[12])
    load_k = [
        pltpu.make_async_copy(kgrads.at[pl.ds(quarter * i, quarter)], k_v.at[pl.ds(quarter * i, quarter)], load_sem.at[8 + i])
        for i in range(4)
    ]
    load_a, load_m = {}, {}
    for o in X_ORDER:
        at = pl.ds(pl.multiple_of(((x + o) % NX) * BLOCK, BLOCK), BLOCK)
        load_a[o] = pltpu.make_async_copy(acts.at[:, at], a_v.at[o], load_sem.at[o])
        load_m[o] = pltpu.make_async_copy(mom.at[0, at], b_v.at[o], load_sem.at[4 + o])
    loads = [load_q] + load_k
    for o in X_ORDER:
        loads += [load_a[o], load_m[o]]
    for copy in loads[:WINDOW]:
        copy.start()
    waiting = iter(loads[WINDOW:])

    def loaded(copy):
        copy.wait()
        for later in waiting:
            later.start()
            break

    barrier = pltpu.get_barrier_semaphore()
    peers = [(xo, yo, 0, False) for xo in range(NX) for yo in range(NY) if (xo, yo) != (0, 0)]
    peers += [(0, 0, zo, False) for zo in range(1, NZ)] + [(0, 0, 0, True)]
    peers += [(xo, 0, zo, False) for xo in range(1, NX) for zo in sorted(RS_DIRECT + AG_DIRECT)]
    for peer in peers:
        pl.semaphore_signal(barrier, inc=1, device_id=device(*peer), device_id_type=MESH)

    loaded(load_q)
    qh, ql = split(q_v[...])
    q2 = jnp.concatenate([qh, ql], axis=1)
    for i in range(4):
        loaded(load_k[i])
        at = slice(quarter * i, quarter * i + quarter)
        two = dot(k_v[at], q2)
        kq_v[at, :RANK], kq_v[at, RANK:] = split(two[:, :RANK] + two[:, RANK:])
    def slot(zo):
        return (zo + (KEPT - 1) // 2) % NZ

    for o in X_ORDER:
        loaded(load_a[o])
        loaded(load_m[o])
        mh, ml = split(b_v[o])
        two = dot(a_v[o], kq_v[...], TN) + dot(mh, q2)
        p = two[:, :RANK] + (two[:, RANK:] + dot(ml, qh))
        for k in range(NZ):
            p_v[o, slot(k + NZ - z)] = p[PIECE * k : PIECE * k + PIECE]
        if o == X_ORDER[0]:
            pl.semaphore_wait(barrier, len(peers))
        if o:
            send(p_v.at[o, pl.ds(0, KEPT)], x_in.at[o - 1], x_sem, device(xo=o))
        for n, zo in enumerate(RS_DIRECT):
            send(p_v.at[o, slot(zo)], d_in.at[o, n], d_sem, device(xo=o, zo=zo))

    def blend(o):
        b = b_v[o] + dot(a_v[o], k_v[...], TN)
        b_v[o] = b
        bh_v[o], bl_v[o] = split(b)

    for o in BEFORE_X:
        blend(o)

    arrive(x_in, x_sem)
    z_src[...] = (p_v[0, :KEPT] + x_in[0]) + (x_in[1] + x_in[2])
    for n, o in enumerate(RS_STAGED):
        send(z_src.at[slot(o)], z_in.at[n], z_sem, device(zo=o))
    for o in BEFORE_Z:
        blend(o)
    mine = z_src[slot(0)]
    if RS_DIRECT:
        arrive(d_in, d_sem)
        for xo in range(NX):
            for n in range(len(RS_DIRECT)):
                mine = mine + d_in[xo, n]
    if RS_STAGED:
        arrive(z_in, z_sem)
    for n in range(KEPT - 1):
        mine = mine + z_in[n]
    own_v[...] = mine * (1.0 / REPLICAS)
    s_v[0, z] = own_v[...]

    for o in Z_FAR:
        send(own_v, s_v.at[0, z], zag_sem.at[o - 1], device(zo=o))
        if o in AG_DIRECT:
            for xo in (2, 1, 3):
                send(own_v, s_v.at[NX - xo, z], xag_sem.at[NX - xo - 1], device(xo=xo, zo=o))
    for xo in (2, 1, 3):
        send(own_v, s_v.at[NX - xo, z], xag_sem.at[NX - xo - 1], device(xo=xo))
    for o in Z_NEAR:
        at = (z + NZ - o) % NZ
        arrive(s_v.at[0, at], zag_sem.at[o - 1])
        if o in AG_STAGED:
            for xo in (2, 1, 3):
                send(s_v.at[0, at], s_v.at[NX - xo, at], xag_sem.at[NX - xo - 1], device(xo=xo))

    def gram(o):
        s = s_v[o].reshape(BLOCK, RANK)
        g_blk[(x + o) % NX] = lax.dot_general(s, s, TN, precision=HIGH, preferred_element_type=f32)

    def halves(o):
        s2_v[o, :, :RANK], s2_v[o, :, RANK:] = split(s_v[o].reshape(BLOCK, RANK))

    gram(0)
    for o in (0, 1, 3, 2):
        if o:
            arrive(s_v.at[o], xag_sem.at[o - 1])
        halves(o)

    def right(dst, which):
        cols = pl.ds(pl.multiple_of(512 * which, 512), 512)
        s2 = s2_v[...].reshape(ROWS, 2 * RANK)
        big = dot(s2, bh_v[:, :, cols].reshape(ROWS, 512), TN)
        small = dot(s2[:, :RANK], bl_v[:, :, cols].reshape(ROWS, 512), TN)
        u = big[:RANK] + (big[RANK:] + small)
        for b in range(4):
            dst[b] = u[:, 128 * b : 128 * b + 128]

    right(u_out, 1 - core)
    for xo in (2, 1, 3, 0):
        to_x = (x + xo) % NX
        send(u_out.at[to_x], c_in.at[to_x], c_sem.at[xo], device(flip=True))
    for o in (1, 3, 2):
        gram(o)
    mine_at = pl.ds(pl.multiple_of(64 * core, 64), 64)
    other_at = pl.ds(pl.multiple_of(64 * (1 - core), 64), 64)
    g_mine[...] = (g_blk[0] + g_blk[1]) + (g_blk[2] + g_blk[3])
    send(g_mine.at[other_at], g_part, g_sem, device(flip=True))
    right(u_own, core)
    for xo in (2, 1, 3, 0):
        to_x = (x + xo) % NX
        arrive(c_in.at[to_x], c_sem.at[xo])
        tot = u_own[to_x] + c_in[to_x]
        for r in range(4):
            half[to_x, r] = tot[32 * r : 32 * r + 32]
        for yo in (2, 1, 3, 0):
            if (xo, yo) != (0, 0):
                send(half.at[to_x, (y + yo) % NY], xy_in.at[xo * NY + yo - 1], xy_sem, device(xo=xo, yo=yo))
    arrive(g_part, g_sem)
    g_y[y] = g_mine[mine_at] + g_part[...]
    for yo in (2, 1, 3):
        send(g_y.at[y], g_y.at[y], gy_sem.at[yo - 1], device(yo=yo))
    me = x * NY + y
    tot = half[x, y]
    arrive(xy_in, xy_sem)
    for o in range(NX * NY - 1):
        tot = tot + xy_in[o]
    v_in[z] = tot
    for o in Z_FAR:
        send(v_in.at[z], v_in.at[z], v_sem.at[o - 1], device(zo=o))
    for yo in (1, 3, 2):
        arrive(g_y.at[(y + NY - yo) % NY], gy_sem.at[yo - 1])
    g_tot[...] = (g_y[0] + g_y[1]) + (g_y[2] + g_y[3])
    send(g_tot, g_rem, gr_sem, device(flip=True))
    ga[mine_at] = g_tot[...]
    arrive(g_rem, gr_sem)
    ga[other_at] = g_rem[...]
    eye = lax.broadcasted_iota(jnp.int32, (RANK, RANK), 0) == lax.broadcasted_iota(jnp.int32, (RANK, RANK), 1)
    ge[...] = eye.astype(f32)
    eliminate(ga, ge, inv_v, 0, CUT)
    for o in Z_NEAR:
        arrive(v_in.at[(z + NZ - o) % NZ], v_sem.at[o - 1])
    tot = v_in[0]
    for o in range(1, NZ):
        tot = tot + v_in[o]
    u_all[core, me] = tot
    order = sorted(
        ((xo, yo) for xo in range(NX) for yo in range(NY) if (xo, yo) != (0, 0)),
        key=lambda o: -min(o[0], NX - o[0]) - min(o[1], NY - o[1]),
    )
    for xo, yo in order:
        send(u_all.at[core, me], u_all.at[core, me], xyag_sem.at[xo * NY + yo - 1], device(xo=xo, yo=yo))
    send(u_all.at[core, me], u_all.at[core, me], cag_sem, device(flip=True))
    eliminate(ga, ge, inv_v, CUT, RANK)
    inverse = inv_v[...]
    for o in range(NX):
        o_v[o] = lax.dot_general(s_v[o].reshape(BLOCK, RANK), inverse, NT, precision=HIGH, preferred_element_type=f32)
    for xo, yo in reversed(order):
        at = ((x + NX - xo) % NX) * NY + (y + NY - yo) % NY
        arrive(u_all.at[core, at], xyag_sem.at[xo * NY + yo - 1])
        send(u_all.at[core, at], u_all.at[core, at], cag_sem, device(flip=True))

    def finish(which):
        for b in range(4):
            ut = u_all[which, pl.ds(4 * b, 4)].reshape(RANK, 128)
            c_v[4 * which + b] = jnp.dot(inverse, ut, precision=HIGH, preferred_element_type=f32) * (1.0 / REPLICAS)

    finish(core)
    arrive(u_all.at[1 - core], cag_sem)
    finish(1 - core)
    for copy in sends:
        copy.wait_send()


def final_kernel(b_ref, o_ref, c_ref, new_ref, basis_ref, upd_ref, c2_v, cl_v, n_v, new_v, basis_v, upd_v, sem):
    x, z = lax.axis_index("dp") // NZ, lax.axis_index("dp") % NZ
    squares = 0.0
    for b in range(8):
        cols = slice(128 * b, 128 * b + 128)
        v = c_ref[b]
        ch, cl_v[:, cols] = split(v)
        c2_v[:RANK, cols] = ch
        c2_v[RANK:, cols] = ch
        squares = squares + v * v
    copies = []
    for o in range(NX):
        for r in range(0, BLOCK, STORED):
            part = slice(r, r + STORED)
            oh, ol = split(o_ref[o, part])
            feedback = dot(jnp.concatenate([oh, ol], axis=1), c2_v[...]) + dot(oh, cl_v[...])
            new_v[o, part] = b_ref[o, part] - 0.2 * feedback
            at = pl.ds(pl.multiple_of(((x + o) % NX) * BLOCK + r, STORED), STORED)
            copies.append(pltpu.make_async_copy(new_v.at[o, pl.ds(r, STORED)], new_ref.at[0, at], sem.at[len(copies)]))
            copies[-1].start()
    norm = jnp.sqrt(jnp.sum(squares, axis=1, keepdims=True) + 1e-06)
    own_h, own_l = split(o_ref[0, pl.ds(pl.multiple_of(z * PIECE, PIECE), PIECE)])
    for b in range(8):
        n_v[b] = c_ref[b] / norm
        nh, nl = split(n_v[b])
        upd = dot(own_h, nh) + (dot(own_h, nl) + dot(own_l, nh))
        upd_v[:, 128 * b : 128 * b + 128] = (math.sqrt(D * KV / RANK) * upd).astype(bf16)
    copies.append(pltpu.make_async_copy(upd_v, upd_ref, sem.at[len(copies)]))
    copies[-1].start()
    basis_v[...] = n_v[lax.axis_index("rows")].T
    copies.append(pltpu.make_async_copy(basis_v, basis_ref, sem.at[len(copies)]))
    copies[-1].start()
    for copy in copies:
        copy.wait()


def body(activations, key_grads, momentum, basis):
    hbm = pl.BlockSpec(memory_space=pl.ANY)
    vmem = pl.BlockSpec(memory_space=pltpu.VMEM)
    sds = jax.ShapeDtypeStruct
    dma = lambda *n: pltpu.SemaphoreType.DMA(n)
    one = pltpu.SemaphoreType.DMA
    b, o, c = pl.pallas_call(
        main_kernel,
        out_shape=(sds((NX, BLOCK, KV), f32), sds((NX, BLOCK, RANK), f32), sds((8, RANK, 128), f32)),
        in_specs=[pl.BlockSpec(memory_space=pltpu.HBM)] * 4,
        out_specs=(vmem,) * 3,
        scratch_shapes=[
            pltpu.VMEM((NX, TOK, BLOCK), bf16),
            pltpu.VMEM((TOK, KV), bf16),
            pltpu.VMEM((TOK, 2 * RANK), bf16),
            pltpu.VMEM((NX, BLOCK, KV), bf16),
            pltpu.VMEM((NX, BLOCK, KV), bf16),
            pltpu.VMEM((KV, RANK), f32),
            pltpu.VMEM((NX, NZ, PIECE, RANK), f32),
            pltpu.VMEM((NX - 1, KEPT, PIECE, RANK), f32),
            pltpu.VMEM((NX, max(1, len(RS_DIRECT)), PIECE, RANK), f32),
            pltpu.VMEM((KEPT, PIECE, RANK), f32),
            pltpu.VMEM((max(1, KEPT - 1), PIECE, RANK), f32),
            pltpu.VMEM((NX, NZ, PIECE, RANK), f32),
            pltpu.VMEM((NX, BLOCK, 2 * RANK), bf16),
            pltpu.VMEM((NX, RANK, RANK), f32),
            pltpu.VMEM((RANK, RANK), f32),
            pltpu.VMEM((64, RANK), f32),
            pltpu.VMEM((NY, 64, RANK), f32),
            pltpu.VMEM((64, RANK), f32),
            pltpu.VMEM((64, RANK), f32),
            pltpu.VMEM((4, RANK, 128), f32),
            pltpu.VMEM((4, RANK, 128), f32),
            pltpu.VMEM((4, RANK, 128), f32),
            pltpu.VMEM((NX, NY, 32, 128), f32),
            pltpu.VMEM((15, 32, 128), f32),
            pltpu.VMEM((NZ, 32, 128), f32),
            pltpu.VMEM((2, 16, 32, 128), f32),
            pltpu.VMEM((PIECE, RANK), f32),
            pltpu.VMEM((RANK, RANK), f32),
            pltpu.VMEM((RANK, RANK), f32),
            pltpu.VMEM((RANK, RANK), f32),
            dma(13), dma(150), one, one, one, dma(7), dma(3), one, dma(3), one, dma(4), one, dma(7), dma(15), one,
        ],
        compiler_params=pltpu.CompilerParams(collective_id=0, has_side_effects=True, vmem_limit_bytes=36 << 20),
        name="main",
    )(*(pltpu.with_memory_space_constraint(v, pltpu.HBM) for v in (activations, key_grads, momentum, basis)))
    return pl.pallas_call(
        final_kernel,
        out_shape=(sds((1, ROWS, KV), f32), sds((RANK, RANK), f32), sds((PIECE, KV), bf16)),
        in_specs=[vmem] * 3,
        out_specs=(hbm,) * 3,
        scratch_shapes=[
            pltpu.VMEM((2 * RANK, KV), bf16),
            pltpu.VMEM((RANK, KV), bf16),
            pltpu.VMEM((8, RANK, 128), f32),
            pltpu.VMEM((NX, BLOCK, KV), f32),
            pltpu.VMEM((RANK, RANK), f32),
            pltpu.VMEM((PIECE, KV), bf16),
            dma(18),
        ],
        compiler_params=pltpu.CompilerParams(vmem_limit_bytes=16 << 20),
        name="final",
    )(b, o, c)


def solution(mesh):
    in_specs = (P("dp", "rows"), P("dp", None), P("dp", "rows", None), P())
    out_specs = (P("dp", "rows", None), P("rows", None), P(("rows", "dp"), None))
    return jax.shard_map(body, mesh=mesh, in_specs=in_specs, out_specs=out_specs, check_vma=False)
```

```python
import functools
import math

import jax
import jax.numpy as jnp
from jax import lax
from jax.experimental import pallas as pl
from jax.experimental.pallas import tpu as pltpu
from jax.sharding import PartitionSpec as P

D = 8192
KV = 1024
RANK = 128
REPLICAS = 32
NX, NY, NZ = 4, 4, 8
TOK = 2048
ROWS = 1024
BLOCK = ROWS // NX
PIECE = BLOCK // NZ
X_ORDER = (2, 1, 3, 0)
Z_FAR = (4, 3, 5, 2, 6, 1, 7)
Z_NEAR = (1, 7, 2, 6, 3, 5, 4)
RS_DIRECT = (4, 3, 5)
AG_DIRECT = ()
RS_STAGED = tuple(o for o in Z_FAR if o not in RS_DIRECT)
AG_STAGED = tuple(o for o in Z_FAR if o not in AG_DIRECT)
KEPT = NZ - len(RS_DIRECT)
BEFORE_X = (0, 1, 2, 3)
BEFORE_Z = ()
STORED = 128
WINDOW = 6
CUT = 56
f32, bf16 = jnp.float32, jnp.bfloat16
HIGH = lax.Precision.HIGHEST
MESH = pl.DeviceIdType.MESH
TN = (((0,), (0,)), ((), ()))
NT = (((1,), (1,)), ((), ()))


def split(v):
    hi = v.astype(bf16)
    return hi, (v - hi.astype(f32)).astype(bf16)


def dot(a, b, dims=(((1,), (0,)), ((), ()))):
    return lax.dot_general(a, b, dims, preferred_element_type=f32)


def eliminate(a_ref, e_ref, inv_ref, first, last):
    tiles = RANK // 8
    a = {i: a_ref[8 * i : 8 * i + 8] for i in range(first // 8, tiles)}
    e = {i: e_ref[8 * i : 8 * i + 8] for i in range(first // 8, tiles)}
    upper = lax.broadcasted_iota(jnp.int32, (8, 1), 0) >= 4
    for k in range(first, last, 4):
        t, s = divmod(k, 8)
        ra = [a[t][s + j : s + j + 1] for j in range(4)]
        re = [e[t][s + j : s + j + 1] for j in range(4)]
        g = {(i, j): jnp.broadcast_to(ra[i][:, k + j : k + j + 1], (1, RANK)) for i in range(4) for j in range(i, 4)}
        wa, we, low = [None] * 4, [None] * 4, {}
        for j in range(4):
            inv = 1.0 / g[j, j]
            for i in range(j + 1, 4):
                low[i, j] = g[j, i] * inv
                for m in range(i, 4):
                    g[i, m] = g[i, m] - low[i, j] * g[j, m]
            for i in range(j + 1, 4):
                ra[i] = ra[i] - low[i, j] * ra[j]
                re[i] = re[i] - low[i, j] * re[j]
            inv_ref[k + j : k + j + 1] = re[j] / jnp.sqrt(g[j, j])
            wa[j], we[j] = ra[j] * inv, re[j] * inv
        for j in (2, 1, 0):
            for i in range(j + 1, 4):
                wa[j] = wa[j] - low[i, j] * wa[i]
                we[j] = we[j] - low[i, j] * we[i]
        for i in range(t, tiles):
            if i == t and s == 4:
                continue
            m = [a[i][:, k + j : k + j + 1] for j in range(4)]
            if i == t:
                m = [jnp.where(upper, v, 0.0) for v in m]
            a[i] = a[i] - ((m[0] * wa[0] + m[1] * wa[1]) + (m[2] * wa[2] + m[3] * wa[3]))
            e[i] = e[i] - ((m[0] * we[0] + m[1] * we[1]) + (m[2] * we[2] + m[3] * we[3]))
    for i in range(last // 8, tiles):
        a_ref[8 * i : 8 * i + 8] = a[i]
        e_ref[8 * i : 8 * i + 8] = e[i]


def main_kernel(
    acts, kgrads, mom, basis,
    b_v, o_v, c_v,
    a_v, k_v, kq_v, bh_v, bl_v, q_v, p_v, x_in, d_in, z_src, z_in, s_v, s2_v, g_blk, g_mine, g_part, g_y, g_tot, g_rem,
    u_out, u_own, c_in, half, xy_in, v_in, u_all, own_v, ga, ge, inv_v,
    load_sem, send_sem, x_sem, d_sem, z_sem, zag_sem, xag_sem, g_sem, gy_sem, gr_sem, c_sem, xy_sem, v_sem, xyag_sem, cag_sem,
):
    dp = lax.axis_index("dp")
    rows = lax.axis_index("rows")
    x, z = dp // NZ, dp % NZ
    y, core = rows // 2, rows % 2
    sends = []

    def device(xo=0, yo=0, zo=0, flip=False):
        c = 1 - core if flip else core
        return (((x + xo) % NX) * NZ + (z + zo) % NZ, ((y + yo) % NY) * 2 + c)

    def send(src, dst, sem, to):
        copy = pltpu.make_async_remote_copy(
            src_ref=src, dst_ref=dst, send_sem=send_sem.at[len(sends)], recv_sem=sem, device_id=to, device_id_type=MESH
        )
        copy.start()
        sends.append(copy)

    def arrive(dst, sem):
        pltpu.make_async_copy(dst, dst, sem).wait()

    quarter = TOK // 4
    load_q = pltpu.make_async_copy(basis, q_v, load_sem.at[12])
    load_k = [
        pltpu.make_async_copy(kgrads.at[pl.ds(quarter * i, quarter)], k_v.at[pl.ds(quarter * i, quarter)], load_sem.at[8 + i])
        for i in range(4)
    ]
    load_a, load_m = {}, {}
    for o in X_ORDER:
        at = pl.ds(pl.multiple_of(((x + o) % NX) * BLOCK, BLOCK), BLOCK)
        load_a[o] = pltpu.make_async_copy(acts.at[:, at], a_v.at[o], load_sem.at[o])
        load_m[o] = pltpu.make_async_copy(mom.at[0, at], b_v.at[o], load_sem.at[4 + o])
    loads = [load_q] + load_k
    for o in X_ORDER:
        loads += [load_a[o], load_m[o]]
    for copy in loads[:WINDOW]:
        copy.start()
    waiting = iter(loads[WINDOW:])

    def loaded(copy):
        copy.wait()
        for later in waiting:
            later.start()
            break

    barrier = pltpu.get_barrier_semaphore()
    peers = [(xo, yo, 0, False) for xo in range(NX) for yo in range(NY) if (xo, yo) != (0, 0)]
    peers += [(0, 0, zo, False) for zo in range(1, NZ)] + [(0, 0, 0, True)]
    peers += [(xo, 0, zo, False) for xo in range(1, NX) for zo in sorted(RS_DIRECT + AG_DIRECT)]
    for peer in peers:
        pl.semaphore_signal(barrier, inc=1, device_id=device(*peer), device_id_type=MESH)

    loaded(load_q)
    qh, ql = split(q_v[...])
    q2 = jnp.concatenate([qh, ql], axis=1)
    for i in range(4):
        loaded(load_k[i])
        at = slice(quarter * i, quarter * i + quarter)
        two = dot(k_v[at], q2)
        kq_v[at, :RANK], kq_v[at, RANK:] = split(two[:, :RANK] + two[:, RANK:])
    def slot(zo):
        return (zo + (KEPT - 1) // 2) % NZ

    for o in X_ORDER:
        loaded(load_a[o])
        loaded(load_m[o])
        mh, ml = split(b_v[o])
        two = dot(a_v[o], kq_v[...], TN) + dot(mh, q2)
        p = two[:, :RANK] + (two[:, RANK:] + dot(ml, qh))
        for k in range(NZ):
            p_v[o, slot(k + NZ - z)] = p[PIECE * k : PIECE * k + PIECE]
        if o == X_ORDER[0]:
            pl.semaphore_wait(barrier, len(peers))
        if o:
            send(p_v.at[o, pl.ds(0, KEPT)], x_in.at[o - 1], x_sem, device(xo=o))
        for n, zo in enumerate(RS_DIRECT):
            send(p_v.at[o, slot(zo)], d_in.at[o, n], d_sem, device(xo=o, zo=zo))

    def blend(o):
        b = b_v[o] + dot(a_v[o], k_v[...], TN)
        b_v[o] = b
        bh_v[o], bl_v[o] = split(b)

    for o in BEFORE_X:
        blend(o)

    arrive(x_in, x_sem)
    z_src[...] = (p_v[0, :KEPT] + x_in[0]) + (x_in[1] + x_in[2])
    for n, o in enumerate(RS_STAGED):
        send(z_src.at[slot(o)], z_in.at[n], z_sem, device(zo=o))
    for o in BEFORE_Z:
        blend(o)
    mine = z_src[slot(0)]
    if RS_DIRECT:
        arrive(d_in, d_sem)
        for xo in range(NX):
            for n in range(len(RS_DIRECT)):
                mine = mine + d_in[xo, n]
    if RS_STAGED:
        arrive(z_in, z_sem)
    for n in range(KEPT - 1):
        mine = mine + z_in[n]
    own_v[...] = mine * (1.0 / REPLICAS)
    s_v[0, z] = own_v[...]

    for o in Z_FAR:
        send(own_v, s_v.at[0, z], zag_sem.at[o - 1], device(zo=o))
        if o in AG_DIRECT:
            for xo in (2, 1, 3):
                send(own_v, s_v.at[NX - xo, z], xag_sem.at[NX - xo - 1], device(xo=xo, zo=o))
    for xo in (2, 1, 3):
        send(own_v, s_v.at[NX - xo, z], xag_sem.at[NX - xo - 1], device(xo=xo))
    for o in Z_NEAR:
        at = (z + NZ - o) % NZ
        arrive(s_v.at[0, at], zag_sem.at[o - 1])
        if o in AG_STAGED:
            for xo in (2, 1, 3):
                send(s_v.at[0, at], s_v.at[NX - xo, at], xag_sem.at[NX - xo - 1], device(xo=xo))

    def gram(o):
        s = s_v[o].reshape(BLOCK, RANK)
        g_blk[(x + o) % NX] = lax.dot_general(s, s, TN, precision=HIGH, preferred_element_type=f32)

    def halves(o):
        s2_v[o, :, :RANK], s2_v[o, :, RANK:] = split(s_v[o].reshape(BLOCK, RANK))

    gram(0)
    for o in (0, 1, 3, 2):
        if o:
            arrive(s_v.at[o], xag_sem.at[o - 1])
        halves(o)

    def right(dst, which):
        cols = pl.ds(pl.multiple_of(512 * which, 512), 512)
        s2 = s2_v[...].reshape(ROWS, 2 * RANK)
        big = dot(s2, bh_v[:, :, cols].reshape(ROWS, 512), TN)
        small = dot(s2[:, :RANK], bl_v[:, :, cols].reshape(ROWS, 512), TN)
        u = big[:RANK] + (big[RANK:] + small)
        for b in range(4):
            dst[b] = u[:, 128 * b : 128 * b + 128]

    right(u_out, 1 - core)
    for xo in (2, 1, 3, 0):
        to_x = (x + xo) % NX
        send(u_out.at[to_x], c_in.at[to_x], c_sem.at[xo], device(flip=True))
    for o in (1, 3, 2):
        gram(o)
    mine_at = pl.ds(pl.multiple_of(64 * core, 64), 64)
    other_at = pl.ds(pl.multiple_of(64 * (1 - core), 64), 64)
    g_mine[...] = (g_blk[0] + g_blk[1]) + (g_blk[2] + g_blk[3])
    send(g_mine.at[other_at], g_part, g_sem, device(flip=True))
    right(u_own, core)
    for xo in (2, 1, 3, 0):
        to_x = (x + xo) % NX
        arrive(c_in.at[to_x], c_sem.at[xo])
        tot = u_own[to_x] + c_in[to_x]
        for r in range(4):
            half[to_x, r] = tot[32 * r : 32 * r + 32]
        for yo in (2, 1, 3, 0):
            if (xo, yo) != (0, 0):
                send(half.at[to_x, (y + yo) % NY], xy_in.at[xo * NY + yo - 1], xy_sem, device(xo=xo, yo=yo))
    arrive(g_part, g_sem)
    g_y[y] = g_mine[mine_at] + g_part[...]
    for yo in (2, 1, 3):
        send(g_y.at[y], g_y.at[y], gy_sem.at[yo - 1], device(yo=yo))
    me = x * NY + y
    tot = half[x, y]
    arrive(xy_in, xy_sem)
    for o in range(NX * NY - 1):
        tot = tot + xy_in[o]
    v_in[z] = tot
    for o in Z_FAR:
        send(v_in.at[z], v_in.at[z], v_sem.at[o - 1], device(zo=o))
    for yo in (1, 3, 2):
        arrive(g_y.at[(y + NY - yo) % NY], gy_sem.at[yo - 1])
    g_tot[...] = (g_y[0] + g_y[1]) + (g_y[2] + g_y[3])
    send(g_tot, g_rem, gr_sem, device(flip=True))
    ga[mine_at] = g_tot[...]
    arrive(g_rem, gr_sem)
    ga[other_at] = g_rem[...]
    eye = lax.broadcasted_iota(jnp.int32, (RANK, RANK), 0) == lax.broadcasted_iota(jnp.int32, (RANK, RANK), 1)
    ge[...] = eye.astype(f32)
    eliminate(ga, ge, inv_v, 0, CUT)
    for o in Z_NEAR:
        arrive(v_in.at[(z + NZ - o) % NZ], v_sem.at[o - 1])
    tot = v_in[0]
    for o in range(1, NZ):
        tot = tot + v_in[o]
    u_all[core, me] = tot
    order = sorted(
        ((xo, yo) for xo in range(NX) for yo in range(NY) if (xo, yo) != (0, 0)),
        key=lambda o: -min(o[0], NX - o[0]) - min(o[1], NY - o[1]),
    )
    for xo, yo in order:
        send(u_all.at[core, me], u_all.at[core, me], xyag_sem.at[xo * NY + yo - 1], device(xo=xo, yo=yo))
    send(u_all.at[core, me], u_all.at[core, me], cag_sem, device(flip=True))
    eliminate(ga, ge, inv_v, CUT, RANK)
    inverse = inv_v[...]

    def pass_on(first, last):
        for xo, yo in order[::-1][first:last]:
            at = ((x + NX - xo) % NX) * NY + (y + NY - yo) % NY
            arrive(u_all.at[core, at], xyag_sem.at[xo * NY + yo - 1])
            send(u_all.at[core, at], u_all.at[core, at], cag_sem, device(flip=True))

    def orthonormal(o):
        o_v[o] = lax.dot_general(s_v[o].reshape(BLOCK, RANK), inverse, NT, precision=HIGH, preferred_element_type=f32)

    pass_on(0, 4)
    orthonormal(0)
    orthonormal(1)
    pass_on(4, 10)
    orthonormal(2)
    orthonormal(3)
    pass_on(10, 15)

    def finish(which):
        for b in range(4):
            ut = u_all[which, pl.ds(4 * b, 4)].reshape(RANK, 128)
            c_v[4 * which + b] = jnp.dot(inverse, ut, precision=HIGH, preferred_element_type=f32) * (1.0 / REPLICAS)

    finish(core)
    arrive(u_all.at[1 - core], cag_sem)
    finish(1 - core)
    for copy in sends:
        copy.wait_send()


def final_kernel(b_ref, o_ref, c_ref, new_ref, basis_ref, upd_ref, c2_v, cl_v, n_v, new_v, basis_v, upd_v, sem):
    x, z = lax.axis_index("dp") // NZ, lax.axis_index("dp") % NZ
    squares = 0.0
    for b in range(8):
        cols = slice(128 * b, 128 * b + 128)
        v = c_ref[b]
        ch, cl_v[:, cols] = split(v)
        c2_v[:RANK, cols] = ch
        c2_v[RANK:, cols] = ch
        squares = squares + v * v
    copies = []
    for o in range(NX):
        for r in range(0, BLOCK, STORED):
            part = slice(r, r + STORED)
            oh, ol = split(o_ref[o, part])
            feedback = dot(jnp.concatenate([oh, ol], axis=1), c2_v[...]) + dot(oh, cl_v[...])
            new_v[o, part] = b_ref[o, part] - 0.2 * feedback
            at = pl.ds(pl.multiple_of(((x + o) % NX) * BLOCK + r, STORED), STORED)
            copies.append(pltpu.make_async_copy(new_v.at[o, pl.ds(r, STORED)], new_ref.at[0, at], sem.at[len(copies)]))
            copies[-1].start()
    norm = jnp.sqrt(jnp.sum(squares, axis=1, keepdims=True) + 1e-06)
    own_h, own_l = split(o_ref[0, pl.ds(pl.multiple_of(z * PIECE, PIECE), PIECE)])
    for b in range(8):
        n_v[b] = c_ref[b] / norm
        nh, nl = split(n_v[b])
        upd = dot(own_h, nh) + (dot(own_h, nl) + dot(own_l, nh))
        upd_v[:, 128 * b : 128 * b + 128] = (math.sqrt(D * KV / RANK) * upd).astype(bf16)
    copies.append(pltpu.make_async_copy(upd_v, upd_ref, sem.at[len(copies)]))
    copies[-1].start()
    basis_v[...] = n_v[lax.axis_index("rows")].T
    copies.append(pltpu.make_async_copy(basis_v, basis_ref, sem.at[len(copies)]))
    copies[-1].start()
    for copy in copies:
        copy.wait()


def body(activations, key_grads, momentum, basis):
    hbm = pl.BlockSpec(memory_space=pl.ANY)
    vmem = pl.BlockSpec(memory_space=pltpu.VMEM)
    sds = jax.ShapeDtypeStruct
    dma = lambda *n: pltpu.SemaphoreType.DMA(n)
    one = pltpu.SemaphoreType.DMA
    b, o, c = pl.pallas_call(
        main_kernel,
        out_shape=(sds((NX, BLOCK, KV), f32), sds((NX, BLOCK, RANK), f32), sds((8, RANK, 128), f32)),
        in_specs=[pl.BlockSpec(memory_space=pltpu.HBM)] * 4,
        out_specs=(vmem,) * 3,
        scratch_shapes=[
            pltpu.VMEM((NX, TOK, BLOCK), bf16),
            pltpu.VMEM((TOK, KV), bf16),
            pltpu.VMEM((TOK, 2 * RANK), bf16),
            pltpu.VMEM((NX, BLOCK, KV), bf16),
            pltpu.VMEM((NX, BLOCK, KV), bf16),
            pltpu.VMEM((KV, RANK), f32),
            pltpu.VMEM((NX, NZ, PIECE, RANK), f32),
            pltpu.VMEM((NX - 1, KEPT, PIECE, RANK), f32),
            pltpu.VMEM((NX, max(1, len(RS_DIRECT)), PIECE, RANK), f32),
            pltpu.VMEM((KEPT, PIECE, RANK), f32),
            pltpu.VMEM((max(1, KEPT - 1), PIECE, RANK), f32),
            pltpu.VMEM((NX, NZ, PIECE, RANK), f32),
            pltpu.VMEM((NX, BLOCK, 2 * RANK), bf16),
            pltpu.VMEM((NX, RANK, RANK), f32),
            pltpu.VMEM((RANK, RANK), f32),
            pltpu.VMEM((64, RANK), f32),
            pltpu.VMEM((NY, 64, RANK), f32),
            pltpu.VMEM((64, RANK), f32),
            pltpu.VMEM((64, RANK), f32),
            pltpu.VMEM((4, RANK, 128), f32),
            pltpu.VMEM((4, RANK, 128), f32),
            pltpu.VMEM((4, RANK, 128), f32),
            pltpu.VMEM((NX, NY, 32, 128), f32),
            pltpu.VMEM((15, 32, 128), f32),
            pltpu.VMEM((NZ, 32, 128), f32),
            pltpu.VMEM((2, 16, 32, 128), f32),
            pltpu.VMEM((PIECE, RANK), f32),
            pltpu.VMEM((RANK, RANK), f32),
            pltpu.VMEM((RANK, RANK), f32),
            pltpu.VMEM((RANK, RANK), f32),
            dma(13), dma(150), one, one, one, dma(7), dma(3), one, dma(3), one, dma(4), one, dma(7), dma(15), one,
        ],
        compiler_params=pltpu.CompilerParams(collective_id=0, has_side_effects=True, vmem_limit_bytes=36 << 20),
        name="main",
    )(*(pltpu.with_memory_space_constraint(v, pltpu.HBM) for v in (activations, key_grads, momentum, basis)))
    return pl.pallas_call(
        final_kernel,
        out_shape=(sds((1, ROWS, KV), f32), sds((RANK, RANK), f32), sds((PIECE, KV), bf16)),
        in_specs=[vmem] * 3,
        out_specs=(hbm,) * 3,
        scratch_shapes=[
            pltpu.VMEM((2 * RANK, KV), bf16),
            pltpu.VMEM((RANK, KV), bf16),
            pltpu.VMEM((8, RANK, 128), f32),
            pltpu.VMEM((NX, BLOCK, KV), f32),
            pltpu.VMEM((RANK, RANK), f32),
            pltpu.VMEM((PIECE, KV), bf16),
            dma(18),
        ],
        compiler_params=pltpu.CompilerParams(vmem_limit_bytes=16 << 20),
        name="final",
    )(b, o, c)


def solution(mesh):
    in_specs = (P("dp", "rows"), P("dp", None), P("dp", "rows", None), P())
    out_specs = (P("dp", "rows", None), P("rows", None), P(("rows", "dp"), None))
    return jax.shard_map(body, mesh=mesh, in_specs=in_specs, out_specs=out_specs, check_vma=False)
```
